512 devices in a mesh: blk: 128 (over z, x, core), col: 4 (over y).
Axes of the slice: x: 4, y: 4, z: 16, core: 2. Of those that a mesh axis runs over, the one named last changes fastest.
Arguments:
- upper_row: float32 [512, 128, 512], P(None, 'blk', 'col'), may hold values from -0.17 to 4.17, as said below
- lower_row: float32 [512, 128, 512], P(None, 'blk', 'col'), may hold values from -0.1 to 0.1
Outputs:
- new_upper: float32 [512, 128, 512], P(None, 'blk', 'col')
- new_lower: float32 [512, 128, 512], P(None, 'blk', 'col')
The draws below stay inside these ranges and needn't reach their ends.
Inputs may be any that keep to these rules, and one draw needn't show every extreme that they name: Block 0 of upper_row is 4 times the identity plus entries within 0.16 of it; the other blocks hold entries within 0.1.
All inputs are finite; a program needn't handle non-finite values.
Results may differ from the reference program's by a relative error of at most 0.00023.
Values sent between devices are 32-bit elements; how exact they have to be, the bound alone decides.
A program may use at most 64 MiB of HBM per device.

```python
import jax
import jax.numpy as jnp
from jax import lax

BLOCK = 512
STEPS = 1
NBLK = 128


def draw_upper_row(key, part):
    shape_all = (BLOCK, NBLK, BLOCK)
    noise_draw = jnp.clip(jax.random.normal(key, shape_all, jnp.float32), -4.0, 4.0)
    leading = (jnp.arange(NBLK) == 0).astype(jnp.float32)[None, :, None]
    spread = 0.025 + 0.015 * leading
    diagonal = (jnp.arange(BLOCK)[:, None] == jnp.arange(BLOCK)[None, :]).astype(jnp.float32)
    return noise_draw * spread + 4.0 * diagonal[:, None, :] * leading


def draw_lower_row(key, part):
    shape_all = (BLOCK, NBLK, BLOCK)
    noise_key = jax.random.fold_in(key, 11)
    noise_draw = jnp.clip(jax.random.normal(noise_key, shape_all, jnp.float32), -4.0, 4.0)
    return noise_draw * 0.025


def setup_inputs(seed: int = 0) -> dict:
    key_list = jax.random.split(jax.random.key(seed), 3)
    upper_row = draw_upper_row(jax.random.fold_in(key_list[2], 71), 0)
    lower_row = draw_lower_row(jax.random.fold_in(key_list[2], 71), 0)
    return {"upper_row": upper_row, "lower_row": lower_row}


HIGHEST_PREC = lax.Precision.HIGHEST

def product(left_mat, right_mat):
    return jnp.dot(left_mat, right_mat, precision=HIGHEST_PREC, preferred_element_type=jnp.float32)

def inverse_root(matrix, identity):
    first_term = (3.0 * identity - matrix) / 2.0
    second_term = (3.0 * identity - product(matrix, product(first_term, first_term))) / 2.0
    return product(first_term, second_term)

def reference(upper_row, lower_row):
    identity = jnp.eye(BLOCK, dtype=jnp.float32)
    upper_flat = upper_row.reshape(BLOCK, NBLK * BLOCK)
    lower_flat = lower_row.reshape(BLOCK, NBLK * BLOCK)
    for step_index in range(1, STEPS + 1):
        upper_flat = jnp.concatenate([jnp.zeros((BLOCK, BLOCK), jnp.float32), upper_flat[:, :-BLOCK]], axis=1)
        head_upper = upper_flat[:, step_index * BLOCK:(step_index + 1) * BLOCK]
        head_lower = lower_flat[:, step_index * BLOCK:(step_index + 1) * BLOCK]
        norm_scale = jnp.sqrt(jnp.sum(head_upper * head_upper) / BLOCK + 1e-06)
        inverse_one = (2.0 * identity - head_upper / norm_scale) / norm_scale
        inverse_two = product(inverse_one, 2.0 * identity - product(head_upper, inverse_one))
        reflect = product(head_lower, inverse_two)
        left_root = inverse_root(identity - product(reflect.T, reflect), identity)
        right_root = inverse_root(identity - product(reflect, reflect.T), identity)
        next_upper = product(left_root, upper_flat - product(reflect.T, lower_flat))
        next_lower = product(right_root, lower_flat - product(reflect, upper_flat))
        upper_flat, lower_flat = (next_upper, next_lower)
    return (upper_flat.reshape(BLOCK, NBLK, BLOCK), lower_flat.reshape(BLOCK, NBLK, BLOCK))
```

```python
import jax
import jax.numpy as jnp
from jax import lax
from jax.experimental import pallas as pl
from jax.experimental.pallas import tpu as pltpu
from jax.sharding import PartitionSpec as P

MESH_ID = pl.DeviceIdType.MESH
F32 = jnp.float32
BF16 = jnp.bfloat16
B = 512
W = 128
Q = 128
NT = (((1,), (1,)), ((), ()))


def split(value):
    hi = value.astype(BF16)
    lo = (value - hi.astype(F32)).astype(BF16)
    return hi, lo


def left_form(value):
    hi, lo = split(value)
    return jnp.concatenate([hi, lo, hi], axis=1)


def dot_nn(left, right):
    return jnp.dot(left, right, preferred_element_type=F32)


def dot_nt(left, right):
    return lax.dot_general(left, right, NT, preferred_element_type=F32)


def communicate(u_in, l_in, buf, ush, loc, sems):
    blk = lax.axis_index("blk")
    y = lax.axis_index("col")
    z, x, c = blk // 8, (blk // 2) % 4, blk % 2
    a, b = x + c * (y - x), y + c * (x - y)
    rdy_in, rdy_out = sems["rdy_p"], sems["rdy_m"]
    odd = z % 2 == 1
    plus = z < 8

    def dev(zz, xx, yy, cc):
        return ((zz * 4 + xx) * 2 + cc, yy)

    def dev_ab(aa, bb):
        return dev(z, aa + c * (bb - aa), bb + c * (aa - bb), c)

    def region(aa, bb, start=0, rows=Q):
        yy, qq = bb + c * (aa - bb), aa + c * (bb - aa)
        return buf.at[c, yy, pl.ds(qq * Q + start, rows), :]

    pending = []

    def send(src, dst, send_sem, recv_sem, device):
        copy = pltpu.make_async_remote_copy(
            src_ref=src, dst_ref=dst, send_sem=send_sem, recv_sem=recv_sem,
            device_id=device, device_id_type=MESH_ID,
        )
        copy.start()
        return copy

    def arrived(dst, recv_sem):
        pltpu.make_async_copy(dst, dst, recv_sem).wait()

    bar = pltpu.get_barrier_semaphore()

    def hello(device):
        pl.semaphore_signal(bar, inc=1, device_id=device, device_id_type=MESH_ID)

    for d in (1, 2, 3):
        hello(dev_ab((a + d) % 4, b))
        hello(dev_ab(a, (b + d) % 4))
    hello(dev(z, x, y, 1 - c))
    gets_shift = jnp.logical_and(c == 0, blk > 0)
    sends_far = jnp.logical_and(c == 1, blk < 127)
    hub_relays = jnp.logical_and(odd, z != 9)

    @pl.when(gets_shift)
    def _():
        hello((blk - 1, y))

    @pl.when(z == 0)
    def _():
        hello(dev(1, x, y, c))
        hello(dev(15, x, y, c))

    @pl.when(jnp.logical_and(odd, z < 7))
    def _():
        hello(dev(z + 2, x, y, c))

    @pl.when(jnp.logical_and(odd, z > 9))
    def _():
        hello(dev(z - 2, x, y, c))

    even_far = jnp.logical_and(z % 2 == 0, z > 0)

    @pl.when(jnp.logical_and(even_far, z <= 8))
    def _():
        hello(dev(z - 1, x, y, c))

    @pl.when(jnp.logical_and(even_far, z > 8))
    def _():
        hello(dev(z + 1, x, y, c))

    local_l = pltpu.make_async_copy(l_in, loc, sems["loc"])
    local_l.start()
    pl.semaphore_wait(
        bar, 7 + sends_far.astype(jnp.int32) + odd.astype(jnp.int32) + hub_relays.astype(jnp.int32)
    )

    @pl.when(jnp.logical_and(odd, z < 8))
    def _():
        @pl.when(z < 7)
        def _():
            pl.semaphore_wait(sems["rdy_p"], 1)

        pl.semaphore_signal(
            sems["rdy_p"], inc=1, device_id=dev(jnp.maximum(z - 2, 0), x, y, c), device_id_type=MESH_ID
        )

    @pl.when(jnp.logical_and(odd, z > 8))
    def _():
        @pl.when(z > 9)
        def _():
            pl.semaphore_wait(sems["rdy_m"], 1)

        pl.semaphore_signal(
            sems["rdy_m"], inc=1, device_id=dev((z + 2 - (z // 15)) % 16, x, y, c), device_id_type=MESH_ID
        )

    shift = pltpu.make_async_remote_copy(
        src_ref=u_in, dst_ref=ush, send_sem=sems["sh_s"], recv_sem=sems["sh_r"],
        device_id=(jnp.minimum(blk + 1, 127), y), device_id_type=MESH_ID,
    )
    has_next = blk < 127

    @pl.when(jnp.logical_and(z > 0, has_next))
    def _():
        shift.start()

    own = region(a, b)
    root = jnp.logical_and(z == 0, x == 0)

    def scatter_from(src_ref):
        for d in (2, 1, 3):
            rows = pl.ds(d * Q, Q)
            send(src_ref.at[rows, :], buf.at[c, y, rows, :], sems["a_s"].at[d - 1], sems["own_r"],
                 dev(0, d, y, c))
        pltpu.make_async_copy(src_ref.at[pl.ds(0, Q), :], buf.at[c, y, pl.ds(0, Q), :], sems["own_r"]).start()

    @pl.when(jnp.logical_and(root, c == 0))
    def _():
        scatter_from(u_in)

    @pl.when(jnp.logical_and(root, c == 1))
    def _():
        scatter_from(l_in)

    arrived(own, sems["own_r"])

    @pl.when(z == 0)
    def _():
        pl.semaphore_wait(sems["rdy_p"], 1)
        pl.semaphore_wait(sems["rdy_m"], 1)
        for i, h in enumerate((7, 5, 3, 1)):
            send(own, own, sems["b_s"].at[i], sems["own_r"], dev(h, x, y, c))
            send(own, own, sems["b_s"].at[4 + i], sems["own_r"], dev(16 - h, x, y, c))

    @pl.when(hub_relays)
    def _():
        send(own, own, sems["b_s"].at[0], sems["own_r"], dev(z + 1 - 2 * (z // 8), x, y, c))

    def to_a(d):
        send(own, own, sems["c1_s"].at[d - 1], sems["c1_r"].at[d - 1], dev_ab((a + d) % 4, b))

    def to_b(j):
        piece = region((a + 4 - j) % 4, b)
        send(piece, piece, sems["fp_s"].at[j], sems["fp_r"].at[j], dev_ab(a, (b + 1) % 4))
        send(piece, piece, sems["fm_s"].at[j], sems["fm_r"].at[j], dev_ab(a, (b + 3) % 4))

    def to_partner(aa, bb, index):
        piece = region(aa, bb)
        send(piece, piece, sems["pt_s"].at[index], sems["pt_r"].at[index], dev(z, x, y, 1 - c))

    def relay(j):
        aj = (a + 4 - j) % 4
        arrived(region(aj, (b + 3) % 4), sems["fp_r"].at[j])
        half = region(aj, (b + 3) % 4, 0, Q // 2)
        send(half, half, sems["hp_s"].at[j], sems["hp_r"].at[j], dev_ab(a, (b + 1) % 4))
        arrived(region(aj, (b + 1) % 4), sems["fm_r"].at[j])
        half = region(aj, (b + 1) % 4, Q // 2, Q // 2)
        send(half, half, sems["hm_s"].at[j], sems["hm_r"].at[j], dev_ab(a, (b + 3) % 4))
        to_partner(aj, (b + 3) % 4, 4 + j)
        to_partner(aj, (b + 1) % 4, 8 + j)

    def took_a(d):
        arrived(region((a + 4 - d) % 4, b), sems["c1_r"].at[d - 1])
        to_b(d)
        to_partner((a + 4 - d) % 4, b, d)

    for d in (2, 1, 3):
        to_a(d)
    to_b(0)
    to_partner(a, b, 0)

    @pl.when(jnp.logical_and(z == 0, has_next))
    def _():
        shift.start()

    @pl.when(blk == 0)
    def _():
        ush[...] = jnp.zeros_like(ush)

    took_a(1)
    took_a(3)
    relay(0)
    took_a(2)
    for j in (1, 3, 2):
        relay(j)
    for j in (0, 1, 3, 2):
        aj, bb = (a + 4 - j) % 4, (b + 2) % 4
        arrived(region(aj, bb, 0, Q // 2), sems["hp_r"].at[j])
        arrived(region(aj, bb, Q // 2, Q // 2), sems["hm_r"].at[j])
        to_partner(aj, bb, 12 + j)

    local_l.wait()

    @pl.when(blk > 0)
    def _():
        arrived(ush, sems["sh_r"])

    e = 1 - c
    pa, pb = x + e * (y - x), y + e * (x - y)
    for index in range(16):
        j, s = index % 4, (0, 3, 1, 2)[index // 4]
        aa, bb = (pa + 4 - j) % 4, (pb + s) % 4
        yy, qq = bb + e * (aa - bb), aa + e * (bb - aa)
        arrived(buf.at[e, yy, pl.ds(qq * Q, Q), :], sems["pt_r"].at[index])

    def finish():
        def sent(ref, sem):
            pltpu.make_async_copy(ref, ref, sem).wait()

        full, half = region(0, 0), region(0, 0, 0, Q // 2)
        for j in range(4):
            sent(full, sems["fp_s"].at[j])
            sent(full, sems["fm_s"].at[j])
            sent(half, sems["hp_s"].at[j])
            sent(half, sems["hm_s"].at[j])
        for j in range(3):
            sent(full, sems["c1_s"].at[j])
        for j in range(16):
            sent(full, sems["pt_s"].at[j])

        @pl.when(root)
        def _():
            for j in range(3):
                sent(full, sems["a_s"].at[j])

        @pl.when(z == 0)
        def _():
            for j in range(8):
                sent(full, sems["b_s"].at[j])

        @pl.when(hub_relays)
        def _():
            sent(full, sems["b_s"].at[0])

        @pl.when(has_next)
        def _():
            sent(ush, sems["sh_s"])

    finish()


def compute(buf, ush, loc, u_out, l_out, n_l, n_r, g_l, h_f, h_l, m_r, k_l, k_n, k_t, d_r):
    rows = lax.broadcasted_iota(jnp.int32, (B, W), 0)
    cols = lax.broadcasted_iota(jnp.int32, (B, W), 1)
    total = jnp.zeros((1, 1), F32)
    for y in range(4):
        f = buf[0, y]
        total = total + jnp.sum(f * f, keepdims=True)
    scale = jnp.sqrt(total / B + 1e-06)
    inv = 1.0 / scale

    def put_left(ref, span, value_hi, value_lo, at):
        ref[span, pl.ds(at, W)] = value_hi
        ref[span, pl.ds(B + at, W)] = value_lo
        ref[span, pl.ds(2 * B + at, W)] = value_hi

    whole = pl.ds(0, B)
    for y in range(4):
        at = y * W
        n = jnp.where(rows == cols + at, 1.0, 0.0) - buf[0, y] * inv
        hi, lo = split(n)
        put_left(n_l, whole, hi, lo, at)
        n_r[pl.ds(0, B), pl.ds(at, W)] = hi
        n_r[pl.ds(B, B), pl.ds(at, W)] = hi
        n_r[pl.ds(2 * B, B), pl.ds(at, W)] = lo
        hi, lo = split(buf[1, y])
        put_left(g_l, whole, hi, lo, at)

    step = 256

    def first(i, carry):
        at = pl.multiple_of(i * step, step)
        span = pl.ds(at, step)
        g = jnp.concatenate([buf[1, y, span, :] for y in range(4)], axis=1)
        h = g + dot_nn(g_l[span, :], n_r[...])
        h_f[span, :] = h
        h_l[span, :] = left_form(h)
        hi, lo = split(dot_nn(n_l[span, :], n_r[...]))
        m_r[span, :] = hi
        m_r[pl.ds(B + at, step), :] = hi
        m_r[pl.ds(2 * B + at, step), :] = lo
        return carry

    lax.fori_loop(0, B // step, first, 0)

    def second(i, carry):
        at = pl.multiple_of(i * step, step)
        span = pl.ds(at, step)
        k = (h_f[span, :] + dot_nn(h_l[span, :], m_r[...])) * inv
        hi, lo = split(k)
        k_n[span, :] = hi
        k_n[pl.ds(B + at, step), :] = hi
        k_n[pl.ds(2 * B + at, step), :] = lo
        k_l[span, :] = jnp.concatenate([hi, lo, hi], axis=1)
        k_t[span, :] = jnp.concatenate([hi, hi, lo], axis=1)
        return carry

    lax.fori_loop(0, B // step, second, 0)

    def third(i, carry):
        at = pl.multiple_of(i * step, step)
        span = pl.ds(at, step)
        hi, lo = split(dot_nt(k_l[span, :], k_t[...]))
        d_r[span, :] = hi
        d_r[pl.ds(B + at, step), :] = hi
        d_r[pl.ds(2 * B + at, step), :] = lo
        return carry

    lax.fori_loop(0, B // step, third, 0)

    low = loc[...].T
    up = ush[...].T
    mixed = up - dot_nn(left_form(low), k_n[...])
    rest = low - dot_nt(left_form(up), k_t[...])
    pulled = dot_nt(left_form(mixed), k_t[...])
    both = jnp.concatenate([rest, pulled], axis=0)
    part = 0.3125 * both + 0.0625 * dot_nn(left_form(both), d_r[...])
    part = 0.375 * both + dot_nn(left_form(part), d_r[...])
    part = 0.5 * both + dot_nn(left_form(part), d_r[...])
    u_out[...] = (mixed + dot_nn(left_form(part[W:]), k_n[...])).T
    l_out[...] = (rest + dot_nn(left_form(part[:W]), d_r[...])).T


SEMS = {
    "rdy_p": None, "rdy_m": None, "loc": (), "sh_s": (), "sh_r": (), "own_r": (),
    "a_s": (3,), "b_s": (8,), "c1_s": (3,), "c1_r": (3,),
    "fp_s": (4,), "fp_r": (4,), "fm_s": (4,), "fm_r": (4,),
    "hp_s": (4,), "hp_r": (4,), "hm_s": (4,), "hm_r": (4,),
    "pt_s": (16,), "pt_r": (16,),
}


def kernel(u_in, l_in, u_out, l_out, buf, ush, loc, *rest):
    mats, sems = rest[:10], dict(zip(SEMS, rest[10:]))
    communicate(u_in, l_in, buf, ush, loc, sems)
    compute(buf, ush, loc, u_out, l_out, *mats)


def shards(upper_row, lower_row):
    shape = jax.ShapeDtypeStruct((B, W), F32)
    cat_l, cat_r = pltpu.VMEM((B, 3 * B), BF16), pltpu.VMEM((3 * B, B), BF16)
    sems = [
        pltpu.SemaphoreType.REGULAR if s is None else pltpu.SemaphoreType.DMA(s) for s in SEMS.values()
    ]
    new_upper, new_lower = pl.pallas_call(
        kernel,
        out_shape=(shape, shape),
        in_specs=[pl.BlockSpec(memory_space=pl.ANY)] * 2,
        out_specs=[pl.BlockSpec(memory_space=pltpu.VMEM)] * 2,
        scratch_shapes=[
            pltpu.VMEM((2, 4, B, W), F32), pltpu.VMEM((B, W), F32), pltpu.VMEM((B, W), F32),
            cat_l, cat_r, cat_l, pltpu.VMEM((B, B), F32), cat_l, cat_r, cat_l, cat_r, cat_l, cat_r,
            *sems,
        ],
        compiler_params=pltpu.CompilerParams(
            collective_id=0, has_side_effects=True, vmem_limit_bytes=56 * 1024 * 1024
        ),
        name="schur",
    )(upper_row.reshape(B, W), lower_row.reshape(B, W))
    return new_upper.reshape(B, 1, W), new_lower.reshape(B, 1, W)


def solution(mesh):
    spec = P(None, "blk", "col")
    return jax.shard_map(
        shards, mesh=mesh, in_specs=(spec, spec), out_specs=(spec, spec), check_vma=False
    )
```

```python
import jax
import jax.numpy as jnp
from jax import lax
from jax.experimental import pallas as pl
from jax.experimental.pallas import tpu as pltpu
from jax.sharding import PartitionSpec as P

MESH_ID = pl.DeviceIdType.MESH
F32 = jnp.float32
BF16 = jnp.bfloat16
B = 512
W = 128
Q = 128
NT = (((1,), (1,)), ((), ()))


def split(value):
    hi = value.astype(BF16)
    lo = (value - hi.astype(F32)).astype(BF16)
    return hi, lo


def left_form(value):
    hi, lo = split(value)
    return jnp.concatenate([hi, lo, hi], axis=1)


def dot_nn(left, right):
    return jnp.dot(left, right, preferred_element_type=F32)


def dot_nt(left, right):
    return lax.dot_general(left, right, NT, preferred_element_type=F32)


def communicate(u_in, l_in, buf, ush, loc, sems):
    blk = lax.axis_index("blk")
    y = lax.axis_index("col")
    z, x, c = blk // 8, (blk // 2) % 4, blk % 2
    a, b = x + c * (y - x), y + c * (x - y)
    odd = z % 2 == 1
    plus = z < 8

    def dev(zz, xx, yy, cc):
        return ((zz * 4 + xx) * 2 + cc, yy)

    def dev_ab(aa, bb):
        return dev(z, aa + c * (bb - aa), bb + c * (aa - bb), c)

    def region(aa, bb, start=0, rows=Q):
        yy, qq = bb + c * (aa - bb), aa + c * (bb - aa)
        return buf.at[c, yy, pl.ds(qq * Q + start, rows), :]

    pending = []

    def send(src, dst, send_sem, recv_sem, device):
        copy = pltpu.make_async_remote_copy(
            src_ref=src, dst_ref=dst, send_sem=send_sem, recv_sem=recv_sem,
            device_id=device, device_id_type=MESH_ID,
        )
        copy.start()
        return copy

    def arrived(dst, recv_sem):
        pltpu.make_async_copy(dst, dst, recv_sem).wait()

    bar = pltpu.get_barrier_semaphore()
    first = jnp.logical_and(blk == 0, y == 0)
    proxy = jnp.logical_and(blk == 1, y == 0)
    column = jnp.logical_and(x == 0, y == 0)
    head = jnp.logical_and(z == 0, jnp.logical_not(first))
    near_row = jnp.logical_and(c == 0, (x == 0) != (y == 0))
    near = jnp.logical_and(z == 0, jnp.logical_or(near_row, jnp.logical_and(c == 1, column)))
    gets_far = jnp.logical_and(c == 0, blk > 0)
    sends_far = jnp.logical_and(c == 1, blk < 127)
    has_next = blk < 127
    relays = jnp.logical_and(odd, z != 9)
    relay_z = z + 1 - 2 * (z // 8)
    even_far = jnp.logical_and(z % 2 == 0, z > 0)
    inner_z = z - 1 + 2 * ((z - 1) // 8)

    def signal(sem, device):
        pl.semaphore_signal(sem, inc=1, device_id=device, device_id_type=MESH_ID)

    def each_peer(act):
        for d in (1, 2, 3):
            act(dev_ab((a + d) % 4, b))
            act(dev_ab(a, (b + d) % 4))
        act(dev(z, x, y, 1 - c))

    @pl.when(jnp.logical_not(first))
    def _():
        each_peer(lambda device: signal(bar, device))

    @pl.when(sends_far)
    def _():
        signal(bar, (blk + 1, y))

    @pl.when(head)
    def _():
        for h in HUBS:
            signal(bar, dev(h, x, y, c))

    @pl.when(proxy)
    def _():
        for h in HUBS:
            signal(bar, dev(h, x, y, 0))

    @pl.when(relays)
    def _():
        signal(bar, dev(relay_z, x, y, c))

    local_l = pltpu.make_async_copy(l_in, loc, sems["loc"])
    local_l.start()
    pl.semaphore_wait(
        bar, 7 - near.astype(jnp.int32) + gets_far.astype(jnp.int32) + (z > 0).astype(jnp.int32)
    )

    @pl.when(first)
    def _():
        each_peer(lambda device: signal(sems["late"], device))

    @pl.when(odd)
    def _():
        lone = jnp.logical_and(column, c == 0).astype(jnp.int32)
        index = jnp.where(plus, z // 2, 4 + (15 - z) // 2) + 8 * lone
        signal(sems["crd"].at[index], dev(0, x, y, c + lone))

    @pl.when(even_far)
    def _():
        signal(sems["rc"], dev(inner_z, x, y, c))

    @pl.when(gets_far)
    def _():
        signal(sems["sh_c"], (blk - 1, y))

    shift = pltpu.make_async_remote_copy(
        src_ref=u_in, dst_ref=ush, send_sem=sems["sh_s"], recv_sem=sems["sh_r"],
        device_id=(jnp.minimum(blk + 1, 127), y), device_id_type=MESH_ID,
    )

    own = region(a, b)
    root = jnp.logical_and(z == 0, x == 0)

    def scatter_from(src_ref):
        for d in (2, 1, 3):
            rows = pl.ds(d * Q, Q)
            send(src_ref.at[rows, :], buf.at[c, y, rows, :], sems["a_s"].at[d - 1], sems["own_r"],
                 dev(0, d, y, c))
        pltpu.make_async_copy(src_ref.at[pl.ds(0, Q), :], buf.at[c, y, pl.ds(0, Q), :], sems["own_r"]).start()

    @pl.when(jnp.logical_and(root, c == 0))
    def _():
        scatter_from(u_in)

    @pl.when(jnp.logical_and(root, c == 1))
    def _():
        scatter_from(l_in)

    arrived(own, sems["own_r"])

    lone_piece = buf.at[0, 0, pl.ds(0, Q), :]

    def to_hubs(piece, core, base, picks):
        for i in picks:
            pl.semaphore_wait(sems["crd"].at[base + i], 1)
            send(piece, piece, sems["b_s"].at[base + i], sems["own_r"], dev(HUBS[i], x, y, core))

    @pl.when(head)
    def _():
        for n, picks in enumerate(((0, 1, 2), (4, 5, 6), (3, 7))):
            to_hubs(own, c, 0, picks)

            @pl.when(proxy)
            def _():
                if n == 0:
                    arrived(lone_piece, sems["pt_r"].at[0])
                to_hubs(lone_piece, 0, 8, picks)

    @pl.when(relays)
    def _():
        pl.semaphore_wait(sems["rc"], 1)
        send(own, own, sems["b_s"].at[0], sems["own_r"], dev(relay_z, x, y, c))

    def to_a(d):
        send(own, own, sems["c1_s"].at[d - 1], sems["c1_r"].at[d - 1], dev_ab((a + d) % 4, b))

    def to_b(j):
        piece = region((a + 4 - j) % 4, b)
        send(piece, piece, sems["fp_s"].at[j], sems["fp_r"].at[j], dev_ab(a, (b + 1) % 4))
        send(piece, piece, sems["fm_s"].at[j], sems["fm_r"].at[j], dev_ab(a, (b + 3) % 4))

    def to_partner(aa, bb, index):
        piece = region(aa, bb)
        send(piece, piece, sems["pt_s"].at[index], sems["pt_r"].at[index], dev(z, x, y, 1 - c))

    def relay(j):
        aj = (a + 4 - j) % 4
        arrived(region(aj, (b + 3) % 4), sems["fp_r"].at[j])
        half = region(aj, (b + 3) % 4, 0, Q // 2)
        send(half, half, sems["hp_s"].at[j], sems["hp_r"].at[j], dev_ab(a, (b + 1) % 4))
        arrived(region(aj, (b + 1) % 4), sems["fm_r"].at[j])
        half = region(aj, (b + 1) % 4, Q // 2, Q // 2)
        send(half, half, sems["hm_s"].at[j], sems["hm_r"].at[j], dev_ab(a, (b + 3) % 4))
        to_partner(aj, (b + 3) % 4, 4 + j)
        to_partner(aj, (b + 1) % 4, 8 + j)

    def took_a(d):
        arrived(region((a + 4 - d) % 4, b), sems["c1_r"].at[d - 1])
        to_b(d)
        to_partner((a + 4 - d) % 4, b, d)

    @pl.when(near)
    def _():
        pl.semaphore_wait(sems["late"], 1)

    to_partner(a, b, 0)
    for d in (2, 1, 3):
        to_a(d)
    to_b(0)

    @pl.when(sends_far)
    def _():
        pl.semaphore_wait(sems["sh_c"], 1)

    @pl.when(has_next)
    def _():
        shift.start()

    @pl.when(blk == 0)
    def _():
        ush[...] = jnp.zeros_like(ush)

    took_a(1)
    took_a(3)
    relay(0)
    took_a(2)
    for j in (1, 3, 2):
        relay(j)
    for j in (0, 1, 3, 2):
        aj, bb = (a + 4 - j) % 4, (b + 2) % 4
        arrived(region(aj, bb, 0, Q // 2), sems["hp_r"].at[j])
        arrived(region(aj, bb, Q // 2, Q // 2), sems["hm_r"].at[j])
        to_partner(aj, bb, 12 + j)

    local_l.wait()

    @pl.when(blk > 0)
    def _():
        arrived(ush, sems["sh_r"])

    e = 1 - c
    pa, pb = x + e * (y - x), y + e * (x - y)
    for index in range(16):
        j, s = index % 4, (0, 3, 1, 2)[index // 4]
        aa, bb = (pa + 4 - j) % 4, (pb + s) % 4
        yy, qq = bb + e * (aa - bb), aa + e * (bb - aa)
        piece = buf.at[e, yy, pl.ds(qq * Q, Q), :]
        if index == 0:

            @pl.when(jnp.logical_not(proxy))
            def _():
                arrived(piece, sems["pt_r"].at[index])
        else:
            arrived(piece, sems["pt_r"].at[index])

    def finish():
        def sent(ref, sem):
            pltpu.make_async_copy(ref, ref, sem).wait()

        full, half = region(0, 0), region(0, 0, 0, Q // 2)
        for j in range(4):
            sent(full, sems["fp_s"].at[j])
            sent(full, sems["fm_s"].at[j])
            sent(half, sems["hp_s"].at[j])
            sent(half, sems["hm_s"].at[j])
        for j in range(3):
            sent(full, sems["c1_s"].at[j])
        for j in range(16):
            sent(full, sems["pt_s"].at[j])

        @pl.when(root)
        def _():
            for j in range(3):
                sent(full, sems["a_s"].at[j])

        @pl.when(head)
        def _():
            for j in range(8):
                sent(full, sems["b_s"].at[j])

        @pl.when(proxy)
        def _():
            for j in range(8, 16):
                sent(full, sems["b_s"].at[j])

        @pl.when(relays)
        def _():
            sent(full, sems["b_s"].at[0])

        @pl.when(has_next)
        def _():
            sent(ush, sems["sh_s"])

    finish()


def compute(buf, ush, loc, u_out, l_out, n_l, n_r, g_l, h_f, h_l, m_r, k_l, k_n, k_t, d_r):
    rows = lax.broadcasted_iota(jnp.int32, (B, W), 0)
    cols = lax.broadcasted_iota(jnp.int32, (B, W), 1)
    total = jnp.zeros((1, 1), F32)
    for y in range(4):
        f = buf[0, y]
        total = total + jnp.sum(f * f, keepdims=True)
    scale = jnp.sqrt(total / B + 1e-06)
    inv = 1.0 / scale

    def put_left(ref, span, value_hi, value_lo, at):
        ref[span, pl.ds(at, W)] = value_hi
        ref[span, pl.ds(B + at, W)] = value_lo
        ref[span, pl.ds(2 * B + at, W)] = value_hi

    whole = pl.ds(0, B)
    for y in range(4):
        at = y * W
        n = jnp.where(rows == cols + at, 1.0, 0.0) - buf[0, y] * inv
        hi, lo = split(n)
        put_left(n_l, whole, hi, lo, at)
        n_r[pl.ds(0, B), pl.ds(at, W)] = hi
        n_r[pl.ds(B, B), pl.ds(at, W)] = hi
        n_r[pl.ds(2 * B, B), pl.ds(at, W)] = lo
        hi, lo = split(buf[1, y])
        put_left(g_l, whole, hi, lo, at)

    step = 256

    def first(i, carry):
        at = pl.multiple_of(i * step, step)
        span = pl.ds(at, step)
        g = jnp.concatenate([buf[1, y, span, :] for y in range(4)], axis=1)
        h = g + dot_nn(g_l[span, :], n_r[...])
        h_f[span, :] = h
        h_l[span, :] = left_form(h)
        hi, lo = split(dot_nn(n_l[span, :], n_r[...]))
        m_r[span, :] = hi
        m_r[pl.ds(B + at, step), :] = hi
        m_r[pl.ds(2 * B + at, step), :] = lo
        return carry

    lax.fori_loop(0, B // step, first, 0)

    def second(i, carry):
        at = pl.multiple_of(i * step, step)
        span = pl.ds(at, step)
        k = (h_f[span, :] + dot_nn(h_l[span, :], m_r[...])) * inv
        hi, lo = split(k)
        k_n[span, :] = hi
        k_n[pl.ds(B + at, step), :] = hi
        k_n[pl.ds(2 * B + at, step), :] = lo
        k_l[span, :] = jnp.concatenate([hi, lo, hi], axis=1)
        k_t[span, :] = jnp.concatenate([hi, hi, lo], axis=1)
        return carry

    lax.fori_loop(0, B // step, second, 0)

    def third(i, carry):
        at = pl.multiple_of(i * step, step)
        span = pl.ds(at, step)
        hi, lo = split(dot_nt(k_l[span, :], k_t[...]))
        d_r[span, :] = hi
        d_r[pl.ds(B + at, step), :] = hi
        d_r[pl.ds(2 * B + at, step), :] = lo
        return carry

    lax.fori_loop(0, B // step, third, 0)

    low = loc[...].T
    up = ush[...].T
    mixed = up - dot_nn(left_form(low), k_n[...])
    rest = low - dot_nt(left_form(up), k_t[...])
    pulled = dot_nt(left_form(mixed), k_t[...])
    both = jnp.concatenate([rest, pulled], axis=0)
    part = 0.3125 * both + 0.0625 * dot_nn(left_form(both), d_r[...])
    part = 0.375 * both + dot_nn(left_form(part), d_r[...])
    part = 0.5 * both + dot_nn(left_form(part), d_r[...])
    u_out[...] = (mixed + dot_nn(left_form(part[W:]), k_n[...])).T
    l_out[...] = (rest + dot_nn(left_form(part[:W]), d_r[...])).T


REG, REG16 = "one", "many"
HUBS = (1, 3, 5, 7, 15, 13, 11, 9)
SEMS = {
    "late": REG, "rc": REG, "sh_c": REG, "crd": REG16, "loc": (), "sh_s": (), "sh_r": (), "own_r": (),
    "a_s": (3,), "b_s": (16,), "c1_s": (3,), "c1_r": (3,),
    "fp_s": (4,), "fp_r": (4,), "fm_s": (4,), "fm_r": (4,),
    "hp_s": (4,), "hp_r": (4,), "hm_s": (4,), "hm_r": (4,),
    "pt_s": (16,), "pt_r": (16,),
}


def kernel(u_in, l_in, u_out, l_out, buf, ush, loc, *rest):
    mats, sems = rest[:10], dict(zip(SEMS, rest[10:]))
    communicate(u_in, l_in, buf, ush, loc, sems)
    compute(buf, ush, loc, u_out, l_out, *mats)


def shards(upper_row, lower_row):
    shape = jax.ShapeDtypeStruct((B, W), F32)
    cat_l, cat_r = pltpu.VMEM((B, 3 * B), BF16), pltpu.VMEM((3 * B, B), BF16)
    kinds = {REG: pltpu.SemaphoreType.REGULAR, REG16: pltpu.SemaphoreType.REGULAR((16,))}
    sems = [kinds[s] if s in kinds else pltpu.SemaphoreType.DMA(s) for s in SEMS.values()]
    new_upper, new_lower = pl.pallas_call(
        kernel,
        out_shape=(shape, shape),
        in_specs=[pl.BlockSpec(memory_space=pl.ANY)] * 2,
        out_specs=[pl.BlockSpec(memory_space=pltpu.VMEM)] * 2,
        scratch_shapes=[
            pltpu.VMEM((2, 4, B, W), F32), pltpu.VMEM((B, W), F32), pltpu.VMEM((B, W), F32),
            cat_l, cat_r, cat_l, pltpu.VMEM((B, B), F32), cat_l, cat_r, cat_l, cat_r, cat_l, cat_r,
            *sems,
        ],
        compiler_params=pltpu.CompilerParams(
            collective_id=0, has_side_effects=True, vmem_limit_bytes=56 * 1024 * 1024
        ),
        name="schur",
    )(upper_row.reshape(B, W), lower_row.reshape(B, W))
    return new_upper.reshape(B, 1, W), new_lower.reshape(B, 1, W)


def solution(mesh):
    spec = P(None, "blk", "col")
    return jax.shard_map(
        shards, mesh=mesh, in_specs=(spec, spec), out_specs=(spec, spec), check_vma=False
    )
```

```python
import jax
import jax.numpy as jnp
from jax import lax
from jax.experimental import pallas as pl
from jax.experimental.pallas import tpu as pltpu
from jax.sharding import PartitionSpec as P

MESH_ID = pl.DeviceIdType.MESH
F32 = jnp.float32
BF16 = jnp.bfloat16
B = 512
W = 128
Q = 128
NT = (((1,), (1,)), ((), ()))


def split(value):
    hi = value.astype(BF16)
    lo = (value - hi.astype(F32)).astype(BF16)
    return hi, lo


def left_form(value):
    hi, lo = split(value)
    return jnp.concatenate([hi, lo, hi], axis=1)


def dot_nn(left, right):
    return jnp.dot(left, right, preferred_element_type=F32)


def dot_nt(left, right):
    return lax.dot_general(left, right, NT, preferred_element_type=F32)


def communicate(u_in, l_in, buf, ush, loc, sems):
    blk = lax.axis_index("blk")
    y = lax.axis_index("col")
    z, x, c = blk // 8, (blk // 2) % 4, blk % 2
    a, b = x + c * (y - x), y + c * (x - y)

    def dev(zz, xx, yy, cc):
        return ((zz * 4 + xx) * 2 + cc, yy)

    def dev_ab(aa, bb):
        return dev(z, aa + c * (bb - aa), bb + c * (aa - bb), c)

    def region(aa, bb, start=0, rows=Q):
        yy, qq = bb + c * (aa - bb), aa + c * (bb - aa)
        return buf.at[c, yy, pl.ds(qq * Q + start, rows), :]

    pending = []

    def send(src, dst, send_sem, recv_sem, device):
        copy = pltpu.make_async_remote_copy(
            src_ref=src, dst_ref=dst, send_sem=send_sem, recv_sem=recv_sem,
            device_id=device, device_id_type=MESH_ID,
        )
        copy.start()
        return copy

    def arrived(dst, recv_sem):
        pltpu.make_async_copy(dst, dst, recv_sem).wait()

    bar = pltpu.get_barrier_semaphore()
    first = jnp.logical_and(blk == 0, y == 0)
    proxy = jnp.logical_and(blk == 1, y == 0)
    column = jnp.logical_and(x == 0, y == 0)
    head = jnp.logical_and(z == 0, jnp.logical_not(first))
    near_row = jnp.logical_and(c == 0, (x == 0) != (y == 0))
    near = jnp.logical_and(z == 0, jnp.logical_or(near_row, jnp.logical_and(c == 1, column)))
    gets_far = jnp.logical_and(c == 0, blk > 0)
    sends_far = jnp.logical_and(c == 1, blk < 127)
    has_next = blk < 127
    up = z <= 8
    sign = 1 - 2 * (z // 9)
    dist = jnp.where(up, z, 16 - z)
    far2 = jnp.logical_or(dist == 4, z == 6)
    far1 = jnp.logical_or(jnp.logical_or(dist == 2, dist == 4), z == 6)
    far3 = z == 12
    step_in = jnp.where(z == 9, 3, jnp.where(dist % 2 == 1, 1, jnp.where(dist == 4, 4, 2)))
    parent = (z - sign * step_in + 16) % 16
    slot = jnp.where(step_in >= 3, 0, jnp.where(step_in == 2, 1, 2)) + 3 * (z // 9)

    def signal(sem, device):
        pl.semaphore_signal(sem, inc=1, device_id=device, device_id_type=MESH_ID)

    def each_peer(act):
        for d in (1, 2, 3):
            act(dev_ab((a + d) % 4, b))
            act(dev_ab(a, (b + d) % 4))
        act(dev(z, x, y, 1 - c))

    @pl.when(jnp.logical_not(first))
    def _():
        each_peer(lambda device: signal(bar, device))

    @pl.when(sends_far)
    def _():
        signal(bar, (blk + 1, y))

    @pl.when(head)
    def _():
        for h in HUBS:
            signal(bar, dev(h, x, y, c))

    @pl.when(proxy)
    def _():
        for h in HUBS:
            signal(bar, dev(h, x, y, 0))

    @pl.when(far3)
    def _():
        signal(bar, dev(9, x, y, c))

    @pl.when(far2)
    def _():
        signal(bar, dev(z + 2 * sign, x, y, c))

    @pl.when(far1)
    def _():
        signal(bar, dev(z + sign, x, y, c))

    local_l = pltpu.make_async_copy(l_in, loc, sems["loc"])
    local_l.start()
    pl.semaphore_wait(
        bar, 7 - near.astype(jnp.int32) + gets_far.astype(jnp.int32) + (z > 0).astype(jnp.int32)
    )

    @pl.when(first)
    def _():
        each_peer(lambda device: signal(sems["late"], device))

    @pl.when(z > 0)
    def _():
        lone = jnp.logical_and(jnp.logical_and(column, c == 0), parent == 0).astype(jnp.int32)
        signal(sems["crd"].at[slot + 6 * lone], dev(parent, x, y, c + lone))

    @pl.when(gets_far)
    def _():
        signal(sems["sh_c"], (blk - 1, y))

    shift = pltpu.make_async_remote_copy(
        src_ref=u_in, dst_ref=ush, send_sem=sems["sh_s"], recv_sem=sems["sh_r"],
        device_id=(jnp.minimum(blk + 1, 127), y), device_id_type=MESH_ID,
    )

    def start_shift():
        @pl.when(sends_far)
        def _():
            pl.semaphore_wait(sems["sh_c"], 1)

        @pl.when(has_next)
        def _():
            shift.start()

    @pl.when(z > 0)
    def _():
        start_shift()

    own = region(a, b)
    root = jnp.logical_and(z == 0, x == 0)

    def scatter_from(src_ref):
        for d in (2, 1, 3):
            rows = pl.ds(d * Q, Q)
            send(src_ref.at[rows, :], buf.at[c, y, rows, :], sems["a_s"].at[d - 1], sems["own_r"],
                 dev(0, d, y, c))
        pltpu.make_async_copy(src_ref.at[pl.ds(0, Q), :], buf.at[c, y, pl.ds(0, Q), :], sems["own_r"]).start()

    @pl.when(jnp.logical_and(root, c == 0))
    def _():
        scatter_from(u_in)

    @pl.when(jnp.logical_and(root, c == 1))
    def _():
        scatter_from(l_in)

    arrived(own, sems["own_r"])

    lone_piece = buf.at[0, 0, pl.ds(0, Q), :]

    def to_child(piece, core, base, i, child):
        pl.semaphore_wait(sems["crd"].at[base + i], 1)
        send(piece, piece, sems["b_s"].at[base + i], sems["own_r"], dev(child, x, y, core))

    def from_root(picks):
        for i in picks:
            to_child(own, c, 0, i, HUBS[i])

    def from_proxy(picks):
        for i in picks:
            to_child(lone_piece, 0, 6, i, HUBS[i])

    @pl.when(head)
    def _():
        from_root((0, 1, 2))

    @pl.when(proxy)
    def _():
        arrived(lone_piece, sems["pt_r"].at[0])
        from_proxy((0, 1, 2))

    side = 3 * (z // 9)

    @pl.when(far3)
    def _():
        to_child(own, c, 0, 3, 9)

    @pl.when(far2)
    def _():
        to_child(own, c, 0, 1 + side, z + 2 * sign)

    @pl.when(far1)
    def _():
        to_child(own, c, 0, 2 + side, z + sign)

    def to_a(d):
        send(own, own, sems["c1_s"].at[d - 1], sems["c1_r"].at[d - 1], dev_ab((a + d) % 4, b))

    def to_b(j):
        piece = region((a + 4 - j) % 4, b)
        send(piece, piece, sems["hp_s"].at[j], sems["hp_r"].at[j], dev_ab(a, (b + 2) % 4))
        send(piece, piece, sems["fp_s"].at[j], sems["fp_r"].at[j], dev_ab(a, (b + 1) % 4))
        send(piece, piece, sems["fm_s"].at[j], sems["fm_r"].at[j], dev_ab(a, (b + 3) % 4))

    def to_partner(aa, bb, index):
        piece = region(aa, bb)
        send(piece, piece, sems["pt_s"].at[index], sems["pt_r"].at[index], dev(z, x, y, 1 - c))

    def took_b(j, d, name):
        aj, bd = (a + 4 - j) % 4, (b + 4 - d) % 4
        arrived(region(aj, bd), sems[name].at[j])
        to_partner(aj, bd, 4 * d + j)

    def took_a(d):
        arrived(region((a + 4 - d) % 4, b), sems["c1_r"].at[d - 1])
        to_b(d)
        to_partner((a + 4 - d) % 4, b, d)

    @pl.when(near)
    def _():
        pl.semaphore_wait(sems["late"], 1)

    to_partner(a, b, 0)
    for d in (2, 1, 3):
        to_a(d)
    to_b(0)

    @pl.when(head)
    def _():
        from_root((3, 4, 5))

    @pl.when(proxy)
    def _():
        from_proxy((3, 4, 5))

    @pl.when(z == 0)
    def _():
        start_shift()

    @pl.when(blk == 0)
    def _():
        ush[...] = jnp.zeros_like(ush)

    for d in (3, 1, 2):
        took_a(d)
    for j in (0, 3, 1, 2):
        took_b(j, 1, "fp_r")
        took_b(j, 3, "fm_r")
        took_b(j, 2, "hp_r")

    local_l.wait()

    @pl.when(blk > 0)
    def _():
        arrived(ush, sems["sh_r"])

    e = 1 - c
    pa, pb = x + e * (y - x), y + e * (x - y)
    for index in range(16):
        j, d = index % 4, index // 4
        aa, bb = (pa + 4 - j) % 4, (pb + 4 - d) % 4
        yy, qq = bb + e * (aa - bb), aa + e * (bb - aa)
        piece = buf.at[e, yy, pl.ds(qq * Q, Q), :]
        if index == 0:

            @pl.when(jnp.logical_not(proxy))
            def _():
                arrived(piece, sems["pt_r"].at[index])
        else:
            arrived(piece, sems["pt_r"].at[index])

    def finish():
        def sent(ref, sem):
            pltpu.make_async_copy(ref, ref, sem).wait()

        full = region(0, 0)
        for j in range(4):
            sent(full, sems["fp_s"].at[j])
            sent(full, sems["fm_s"].at[j])
            sent(full, sems["hp_s"].at[j])
        for j in range(3):
            sent(full, sems["c1_s"].at[j])
        for j in range(16):
            sent(full, sems["pt_s"].at[j])

        @pl.when(root)
        def _():
            for j in range(3):
                sent(full, sems["a_s"].at[j])

        @pl.when(head)
        def _():
            for j in range(6):
                sent(full, sems["b_s"].at[j])

        @pl.when(proxy)
        def _():
            for j in range(6, 12):
                sent(full, sems["b_s"].at[j])

        @pl.when(far3)
        def _():
            sent(full, sems["b_s"].at[3])

        @pl.when(far2)
        def _():
            sent(full, sems["b_s"].at[1 + side])

        @pl.when(far1)
        def _():
            sent(full, sems["b_s"].at[2 + side])

        @pl.when(has_next)
        def _():
            sent(ush, sems["sh_s"])

    finish()


def compute(buf, ush, loc, u_out, l_out, n_l, n_r, g_l, h_f, h_l, m_r, k_l, k_n, k_t, d_r):
    rows = lax.broadcasted_iota(jnp.int32, (B, W), 0)
    cols = lax.broadcasted_iota(jnp.int32, (B, W), 1)
    total = jnp.zeros((1, 1), F32)
    for y in range(4):
        f = buf[0, y]
        total = total + jnp.sum(f * f, keepdims=True)
    scale = jnp.sqrt(total / B + 1e-06)
    inv = 1.0 / scale

    def put_left(ref, span, value_hi, value_lo, at):
        ref[span, pl.ds(at, W)] = value_hi
        ref[span, pl.ds(B + at, W)] = value_lo
        ref[span, pl.ds(2 * B + at, W)] = value_hi

    whole = pl.ds(0, B)
    for y in range(4):
        at = y * W
        n = jnp.where(rows == cols + at, 1.0, 0.0) - buf[0, y] * inv
        hi, lo = split(n)
        put_left(n_l, whole, hi, lo, at)
        n_r[pl.ds(0, B), pl.ds(at, W)] = hi
        n_r[pl.ds(B, B), pl.ds(at, W)] = hi
        n_r[pl.ds(2 * B, B), pl.ds(at, W)] = lo
        hi, lo = split(buf[1, y])
        put_left(g_l, whole, hi, lo, at)

    step = 256

    def first(i, carry):
        at = pl.multiple_of(i * step, step)
        span = pl.ds(at, step)
        g = jnp.concatenate([buf[1, y, span, :] for y in range(4)], axis=1)
        h = g + dot_nn(g_l[span, :], n_r[...])
        h_f[span, :] = h
        h_l[span, :] = left_form(h)
        hi, lo = split(dot_nn(n_l[span, :], n_r[...]))
        m_r[span, :] = hi
        m_r[pl.ds(B + at, step), :] = hi
        m_r[pl.ds(2 * B + at, step), :] = lo
        return carry

    lax.fori_loop(0, B // step, first, 0)

    def second(i, carry):
        at = pl.multiple_of(i * step, step)
        span = pl.ds(at, step)
        k = (h_f[span, :] + dot_nn(h_l[span, :], m_r[...])) * inv
        hi, lo = split(k)
        k_n[span, :] = hi
        k_n[pl.ds(B + at, step), :] = hi
        k_n[pl.ds(2 * B + at, step), :] = lo
        k_l[span, :] = jnp.concatenate([hi, lo, hi], axis=1)
        k_t[span, :] = jnp.concatenate([hi, hi, lo], axis=1)
        return carry

    lax.fori_loop(0, B // step, second, 0)

    def third(i, carry):
        at = pl.multiple_of(i * step, step)
        span = pl.ds(at, step)
        hi, lo = split(dot_nt(k_l[span, :], k_t[...]))
        d_r[span, :] = hi
        d_r[pl.ds(B + at, step), :] = hi
        d_r[pl.ds(2 * B + at, step), :] = lo
        return carry

    lax.fori_loop(0, B // step, third, 0)

    low = loc[...].T
    up = ush[...].T
    mixed = up - dot_nn(left_form(low), k_n[...])
    rest = low - dot_nt(left_form(up), k_t[...])
    pulled = dot_nt(left_form(mixed), k_t[...])
    both = jnp.concatenate([rest, pulled], axis=0)
    part = 0.3125 * both + 0.0625 * dot_nn(left_form(both), d_r[...])
    part = 0.375 * both + dot_nn(left_form(part), d_r[...])
    part = 0.5 * both + dot_nn(left_form(part), d_r[...])
    u_out[...] = (mixed + dot_nn(left_form(part[W:]), k_n[...])).T
    l_out[...] = (rest + dot_nn(left_form(part[:W]), d_r[...])).T


REG, REG16 = "one", "many"
HUBS = (4, 2, 1, 12, 14, 15)
SEMS = {
    "late": REG, "sh_c": REG, "crd": REG16, "loc": (), "sh_s": (), "sh_r": (), "own_r": (),
    "a_s": (3,), "b_s": (12,), "c1_s": (3,), "c1_r": (3,),
    "fp_s": (4,), "fp_r": (4,), "fm_s": (4,), "fm_r": (4,),
    "hp_s": (4,), "hp_r": (4,),
    "pt_s": (16,), "pt_r": (16,),
}


def kernel(u_in, l_in, u_out, l_out, buf, ush, loc, *rest):
    mats, sems = rest[:10], dict(zip(SEMS, rest[10:]))
    communicate(u_in, l_in, buf, ush, loc, sems)
    compute(buf, ush, loc, u_out, l_out, *mats)


def shards(upper_row, lower_row):
    shape = jax.ShapeDtypeStruct((B, W), F32)
    cat_l, cat_r = pltpu.VMEM((B, 3 * B), BF16), pltpu.VMEM((3 * B, B), BF16)
    kinds = {REG: pltpu.SemaphoreType.REGULAR, REG16: pltpu.SemaphoreType.REGULAR((16,))}
    sems = [kinds[s] if s in kinds else pltpu.SemaphoreType.DMA(s) for s in SEMS.values()]
    new_upper, new_lower = pl.pallas_call(
        kernel,
        out_shape=(shape, shape),
        in_specs=[pl.BlockSpec(memory_space=pl.ANY)] * 2,
        out_specs=[pl.BlockSpec(memory_space=pltpu.VMEM)] * 2,
        scratch_shapes=[
            pltpu.VMEM((2, 4, B, W), F32), pltpu.VMEM((B, W), F32), pltpu.VMEM((B, W), F32),
            cat_l, cat_r, cat_l, pltpu.VMEM((B, B), F32), cat_l, cat_r, cat_l, cat_r, cat_l, cat_r,
            *sems,
        ],
        compiler_params=pltpu.CompilerParams(
            collective_id=0, has_side_effects=True, vmem_limit_bytes=56 * 1024 * 1024
        ),
        name="schur",
    )(upper_row.reshape(B, W), lower_row.reshape(B, W))
    return new_upper.reshape(B, 1, W), new_lower.reshape(B, 1, W)


def solution(mesh):
    spec = P(None, "blk", "col")
    return jax.shard_map(
        shards, mesh=mesh, in_specs=(spec, spec), out_specs=(spec, spec), check_vma=False
    )
```

```python
import jax
import jax.numpy as jnp
from jax import lax
from jax.experimental import pallas as pl
from jax.experimental.pallas import tpu as pltpu
from jax.sharding import PartitionSpec as P

MESH_ID = pl.DeviceIdType.MESH
F32 = jnp.float32
BF16 = jnp.bfloat16
B = 512
W = 128
Q = 128
NT = (((1,), (1,)), ((), ()))


def split(value):
    hi = value.astype(BF16)
    lo = (value - hi.astype(F32)).astype(BF16)
    return hi, lo


def left_form(value):
    hi, lo = split(value)
    return jnp.concatenate([hi, lo, hi], axis=1)


def dot_nn(left, right):
    return jnp.dot(left, right, preferred_element_type=F32)


def dot_nt(left, right):
    return lax.dot_general(left, right, NT, preferred_element_type=F32)


def prepare(ref, turned, left):
    value = ref[...].T
    turned[...] = value
    left[...] = left_form(value)


def communicate(u_in, l_in, buf, ush, loc, low_t, low_l, up_t, up_l, sems):
    blk = lax.axis_index("blk")
    y = lax.axis_index("col")
    z, x, c = blk // 8, (blk // 2) % 4, blk % 2
    a, b = x + c * (y - x), y + c * (x - y)

    def dev(zz, xx, yy, cc):
        return ((zz * 4 + xx) * 2 + cc, yy)

    def dev_ab(aa, bb):
        return dev(z, aa + c * (bb - aa), bb + c * (aa - bb), c)

    def region(aa, bb, start=0, rows=Q):
        yy, qq = bb + c * (aa - bb), aa + c * (bb - aa)
        return buf.at[c, yy, pl.ds(qq * Q + start, rows), :]

    pending = []

    def send(src, dst, send_sem, recv_sem, device):
        copy = pltpu.make_async_remote_copy(
            src_ref=src, dst_ref=dst, send_sem=send_sem, recv_sem=recv_sem,
            device_id=device, device_id_type=MESH_ID,
        )
        copy.start()
        return copy

    def arrived(dst, recv_sem):
        pltpu.make_async_copy(dst, dst, recv_sem).wait()

    bar = pltpu.get_barrier_semaphore()
    first = jnp.logical_and(blk == 0, y == 0)
    proxy = jnp.logical_and(blk == 1, y == 0)
    column = jnp.logical_and(x == 0, y == 0)
    head = jnp.logical_and(z == 0, jnp.logical_not(first))
    near_row = jnp.logical_and(c == 0, (x == 0) != (y == 0))
    near = jnp.logical_and(z == 0, jnp.logical_or(near_row, jnp.logical_and(c == 1, column)))
    gets_far = jnp.logical_and(c == 0, blk > 0)
    sends_far = jnp.logical_and(c == 1, blk < 127)
    has_next = blk < 127
    up = z <= 8
    sign = 1 - 2 * (z // 9)
    dist = jnp.where(up, z, 16 - z)
    far2 = jnp.logical_or(dist == 4, z == 6)
    far1 = jnp.logical_or(jnp.logical_or(dist == 2, dist == 4), z == 6)
    far3 = z == 12
    step_in = jnp.where(z == 9, 3, jnp.where(dist % 2 == 1, 1, jnp.where(dist == 4, 4, 2)))
    parent = (z - sign * step_in + 16) % 16
    slot = jnp.where(step_in >= 3, 0, jnp.where(step_in == 2, 1, 2)) + 3 * (z // 9)

    def signal(sem, device):
        pl.semaphore_signal(sem, inc=1, device_id=device, device_id_type=MESH_ID)

    def each_peer(act):
        for d in (1, 2, 3):
            act(dev_ab((a + d) % 4, b))
            act(dev_ab(a, (b + d) % 4))
        act(dev(z, x, y, 1 - c))

    @pl.when(jnp.logical_not(first))
    def _():
        each_peer(lambda device: signal(bar, device))

    @pl.when(sends_far)
    def _():
        signal(bar, (blk + 1, y))

    @pl.when(head)
    def _():
        for h in HUBS:
            signal(bar, dev(h, x, y, c))

    @pl.when(proxy)
    def _():
        for h in HUBS:
            signal(bar, dev(h, x, y, 0))

    @pl.when(far3)
    def _():
        signal(bar, dev(9, x, y, c))

    @pl.when(far2)
    def _():
        signal(bar, dev(z + 2 * sign, x, y, c))

    @pl.when(far1)
    def _():
        signal(bar, dev(z + sign, x, y, c))

    local_l = pltpu.make_async_copy(l_in, loc, sems["loc"])
    local_l.start()
    pl.semaphore_wait(
        bar, 7 - near.astype(jnp.int32) + gets_far.astype(jnp.int32) + (z > 0).astype(jnp.int32)
    )

    @pl.when(first)
    def _():
        each_peer(lambda device: signal(sems["late"], device))

    @pl.when(z > 0)
    def _():
        lone = jnp.logical_and(jnp.logical_and(column, c == 0), parent == 0).astype(jnp.int32)
        signal(sems["crd"].at[slot + 6 * lone], dev(parent, x, y, c + lone))

    @pl.when(gets_far)
    def _():
        signal(sems["sh_c"], (blk - 1, y))

    shift = pltpu.make_async_remote_copy(
        src_ref=u_in, dst_ref=ush, send_sem=sems["sh_s"], recv_sem=sems["sh_r"],
        device_id=(jnp.minimum(blk + 1, 127), y), device_id_type=MESH_ID,
    )

    def start_shift():
        @pl.when(sends_far)
        def _():
            pl.semaphore_wait(sems["sh_c"], 1)

        @pl.when(has_next)
        def _():
            shift.start()

    @pl.when(z > 0)
    def _():
        start_shift()

    own = region(a, b)
    root = jnp.logical_and(z == 0, x == 0)

    def scatter_from(src_ref):
        for d in (2, 1, 3):
            rows = pl.ds(d * Q, Q)
            send(src_ref.at[rows, :], buf.at[c, y, rows, :], sems["a_s"].at[d - 1], sems["own_r"],
                 dev(0, d, y, c))
        pltpu.make_async_copy(src_ref.at[pl.ds(0, Q), :], buf.at[c, y, pl.ds(0, Q), :], sems["own_r"]).start()

    @pl.when(jnp.logical_and(root, c == 0))
    def _():
        scatter_from(u_in)

    @pl.when(jnp.logical_and(root, c == 1))
    def _():
        scatter_from(l_in)

    arrived(own, sems["own_r"])

    lone_piece = buf.at[0, 0, pl.ds(0, Q), :]

    def to_child(piece, core, base, i, child):
        pl.semaphore_wait(sems["crd"].at[base + i], 1)
        send(piece, piece, sems["b_s"].at[base + i], sems["own_r"], dev(child, x, y, core))

    def from_root(picks):
        for i in picks:
            to_child(own, c, 0, i, HUBS[i])

    def from_proxy(picks):
        for i in picks:
            to_child(lone_piece, 0, 6, i, HUBS[i])

    @pl.when(head)
    def _():
        from_root((0, 1, 2))

    @pl.when(proxy)
    def _():
        arrived(lone_piece, sems["pt_r"].at[0])
        from_proxy((0, 1, 2))

    side = 3 * (z // 9)

    @pl.when(far3)
    def _():
        to_child(own, c, 0, 3, 9)

    @pl.when(far2)
    def _():
        to_child(own, c, 0, 1 + side, z + 2 * sign)

    @pl.when(far1)
    def _():
        to_child(own, c, 0, 2 + side, z + sign)

    def to_a(d):
        send(own, own, sems["c1_s"].at[d - 1], sems["c1_r"].at[d - 1], dev_ab((a + d) % 4, b))

    def to_b(j):
        piece = region((a + 4 - j) % 4, b)
        send(piece, piece, sems["hp_s"].at[j], sems["hp_r"].at[j], dev_ab(a, (b + 2) % 4))
        send(piece, piece, sems["fp_s"].at[j], sems["fp_r"].at[j], dev_ab(a, (b + 1) % 4))
        send(piece, piece, sems["fm_s"].at[j], sems["fm_r"].at[j], dev_ab(a, (b + 3) % 4))

    def to_partner(aa, bb, index):
        piece = region(aa, bb)
        send(piece, piece, sems["pt_s"].at[index], sems["pt_r"].at[index], dev(z, x, y, 1 - c))

    def took_b(j, d, name):
        aj, bd = (a + 4 - j) % 4, (b + 4 - d) % 4
        arrived(region(aj, bd), sems[name].at[j])
        to_partner(aj, bd, 4 * d + j)

    def took_a(d):
        arrived(region((a + 4 - d) % 4, b), sems["c1_r"].at[d - 1])
        to_b(d)
        to_partner((a + 4 - d) % 4, b, d)

    @pl.when(near)
    def _():
        pl.semaphore_wait(sems["late"], 1)

    to_partner(a, b, 0)
    for d in (2, 1, 3):
        to_a(d)
    to_b(0)

    @pl.when(head)
    def _():
        from_root((3, 4, 5))

    @pl.when(proxy)
    def _():
        from_proxy((3, 4, 5))

    @pl.when(z == 0)
    def _():
        start_shift()

    @pl.when(blk == 0)
    def _():
        ush[...] = jnp.zeros_like(ush)

    local_l.wait()
    prepare(loc, low_t, low_l)
    for d in (3, 1, 2):
        took_a(d)

    @pl.when(blk > 0)
    def _():
        arrived(ush, sems["sh_r"])

    prepare(ush, up_t, up_l)
    for j in (0, 3, 1, 2):
        took_b(j, 1, "fp_r")
        took_b(j, 3, "fm_r")
        took_b(j, 2, "hp_r")

    e = 1 - c
    pa, pb = x + e * (y - x), y + e * (x - y)
    for index in range(16):
        j, d = index % 4, index // 4
        aa, bb = (pa + 4 - j) % 4, (pb + 4 - d) % 4
        yy, qq = bb + e * (aa - bb), aa + e * (bb - aa)
        piece = buf.at[e, yy, pl.ds(qq * Q, Q), :]
        if index == 0:

            @pl.when(jnp.logical_not(proxy))
            def _():
                arrived(piece, sems["pt_r"].at[index])
        else:
            arrived(piece, sems["pt_r"].at[index])

    def finish():
        def sent(ref, sem):
            pltpu.make_async_copy(ref, ref, sem).wait()

        full = region(0, 0)
        for j in range(4):
            sent(full, sems["fp_s"].at[j])
            sent(full, sems["fm_s"].at[j])
            sent(full, sems["hp_s"].at[j])
        for j in range(3):
            sent(full, sems["c1_s"].at[j])
        for j in range(16):
            sent(full, sems["pt_s"].at[j])

        @pl.when(root)
        def _():
            for j in range(3):
                sent(full, sems["a_s"].at[j])

        @pl.when(head)
        def _():
            for j in range(6):
                sent(full, sems["b_s"].at[j])

        @pl.when(proxy)
        def _():
            for j in range(6, 12):
                sent(full, sems["b_s"].at[j])

        @pl.when(far3)
        def _():
            sent(full, sems["b_s"].at[3])

        @pl.when(far2)
        def _():
            sent(full, sems["b_s"].at[1 + side])

        @pl.when(far1)
        def _():
            sent(full, sems["b_s"].at[2 + side])

        @pl.when(has_next)
        def _():
            sent(ush, sems["sh_s"])

    finish()


def compute(buf, low_t, low_l, up_t, up_l, u_out, l_out, n_l, n_r, g_l, h_f, h_l, m_r, k_l, k_n, k_t, d_r):
    rows = lax.broadcasted_iota(jnp.int32, (B, W), 0)
    cols = lax.broadcasted_iota(jnp.int32, (B, W), 1)
    total = jnp.zeros((1, 1), F32)
    for y in range(4):
        f = buf[0, y]
        total = total + jnp.sum(f * f, keepdims=True)
    scale = jnp.sqrt(total / B + 1e-06)
    inv = 1.0 / scale

    def put_left(ref, span, value_hi, value_lo, at):
        ref[span, pl.ds(at, W)] = value_hi
        ref[span, pl.ds(B + at, W)] = value_lo
        ref[span, pl.ds(2 * B + at, W)] = value_hi

    whole = pl.ds(0, B)
    for y in range(4):
        at = y * W
        n = jnp.where(rows == cols + at, 1.0, 0.0) - buf[0, y] * inv
        hi, lo = split(n)
        put_left(n_l, whole, hi, lo, at)
        n_r[pl.ds(0, B), pl.ds(at, W)] = hi
        n_r[pl.ds(B, B), pl.ds(at, W)] = hi
        n_r[pl.ds(2 * B, B), pl.ds(at, W)] = lo
        hi, lo = split(buf[1, y])
        put_left(g_l, whole, hi, lo, at)

    step = 512

    def first(i, carry):
        at = pl.multiple_of(i * step, step)
        span = pl.ds(at, step)
        g = jnp.concatenate([buf[1, y, span, :] for y in range(4)], axis=1)
        h = g + dot_nn(g_l[span, :], n_r[...])
        h_f[span, :] = h
        h_l[span, :] = left_form(h)
        hi, lo = split(dot_nn(n_l[span, :], n_r[...]))
        m_r[span, :] = hi
        m_r[pl.ds(B + at, step), :] = hi
        m_r[pl.ds(2 * B + at, step), :] = lo
        return carry

    lax.fori_loop(0, B // step, first, 0)

    def second(i, carry):
        at = pl.multiple_of(i * step, step)
        span = pl.ds(at, step)
        k = (h_f[span, :] + dot_nn(h_l[span, :], m_r[...])) * inv
        hi, lo = split(k)
        k_n[span, :] = hi
        k_n[pl.ds(B + at, step), :] = hi
        k_n[pl.ds(2 * B + at, step), :] = lo
        k_l[span, :] = jnp.concatenate([hi, lo, hi], axis=1)
        k_t[span, :] = jnp.concatenate([hi, hi, lo], axis=1)
        return carry

    lax.fori_loop(0, B // step, second, 0)

    def third(i, carry):
        at = pl.multiple_of(i * step, step)
        span = pl.ds(at, step)
        hi, lo = split(dot_nt(k_l[span, :], k_t[...]))
        d_r[span, :] = hi
        d_r[pl.ds(B + at, step), :] = hi
        d_r[pl.ds(2 * B + at, step), :] = lo
        return carry

    lax.fori_loop(0, B // step, third, 0)

    mixed = up_t[...] - dot_nn(low_l[...], k_n[...])
    rest = low_t[...] - dot_nt(up_l[...], k_t[...])
    pulled = dot_nt(left_form(mixed), k_t[...])
    both = jnp.concatenate([rest, pulled], axis=0)
    part = 0.3125 * both + 0.0625 * dot_nn(left_form(both), d_r[...])
    part = 0.375 * both + dot_nn(left_form(part), d_r[...])
    part = 0.5 * both + dot_nn(left_form(part), d_r[...])
    u_out[...] = (mixed + dot_nn(left_form(part[W:]), k_n[...])).T
    l_out[...] = (rest + dot_nn(left_form(part[:W]), d_r[...])).T


REG, REG16 = "one", "many"
HUBS = (4, 2, 1, 12, 14, 15)
SEMS = {
    "late": REG, "sh_c": REG, "crd": REG16, "loc": (), "sh_s": (), "sh_r": (), "own_r": (),
    "a_s": (3,), "b_s": (12,), "c1_s": (3,), "c1_r": (3,),
    "fp_s": (4,), "fp_r": (4,), "fm_s": (4,), "fm_r": (4,),
    "hp_s": (4,), "hp_r": (4,),
    "pt_s": (16,), "pt_r": (16,),
}


def kernel(u_in, l_in, u_out, l_out, buf, ush, loc, *rest):
    own, mats, sems = rest[:4], rest[4:14], dict(zip(SEMS, rest[14:]))
    communicate(u_in, l_in, buf, ush, loc, *own, sems)
    compute(buf, *own, u_out, l_out, *mats)


def shards(upper_row, lower_row):
    shape = jax.ShapeDtypeStruct((B, W), F32)
    cat_l, cat_r = pltpu.VMEM((B, 3 * B), BF16), pltpu.VMEM((3 * B, B), BF16)
    kinds = {REG: pltpu.SemaphoreType.REGULAR, REG16: pltpu.SemaphoreType.REGULAR((16,))}
    sems = [kinds[s] if s in kinds else pltpu.SemaphoreType.DMA(s) for s in SEMS.values()]
    new_upper, new_lower = pl.pallas_call(
        kernel,
        out_shape=(shape, shape),
        in_specs=[pl.BlockSpec(memory_space=pl.ANY)] * 2,
        out_specs=[pl.BlockSpec(memory_space=pltpu.VMEM)] * 2,
        scratch_shapes=[
            pltpu.VMEM((2, 4, B, W), F32), pltpu.VMEM((B, W), F32), pltpu.VMEM((B, W), F32),
            *[pltpu.VMEM((W, B), F32), pltpu.VMEM((W, 3 * B), BF16)] * 2,
            cat_l, cat_r, cat_l, pltpu.VMEM((B, B), F32), cat_l, cat_r, cat_l, cat_r, cat_l, cat_r,
            *sems,
        ],
        compiler_params=pltpu.CompilerParams(
            collective_id=0, has_side_effects=True, vmem_limit_bytes=56 * 1024 * 1024
        ),
        name="schur",
    )(upper_row.reshape(B, W), lower_row.reshape(B, W))
    return new_upper.reshape(B, 1, W), new_lower.reshape(B, 1, W)


def solution(mesh):
    spec = P(None, "blk", "col")
    return jax.shard_map(
        shards, mesh=mesh, in_specs=(spec, spec), out_specs=(spec, spec), check_vma=False
    )
```

```python
import jax
import jax.numpy as jnp
from jax import lax
from jax.experimental import pallas as pl
from jax.experimental.pallas import tpu as pltpu
from jax.sharding import PartitionSpec as P

MESH_ID = pl.DeviceIdType.MESH
F32 = jnp.float32
BF16 = jnp.bfloat16
B = 512
W = 128
Q = 128
NT = (((1,), (1,)), ((), ()))


def split(value):
    hi = value.astype(BF16)
    lo = (value - hi.astype(F32)).astype(BF16)
    return hi, lo


def left_form(value):
    hi, lo = split(value)
    return jnp.concatenate([hi, lo, hi], axis=1)


def dot_nn(left, right):
    return jnp.dot(left, right, preferred_element_type=F32)


def dot_nt(left, right):
    return lax.dot_general(left, right, NT, preferred_element_type=F32)


def prepare(ref, turned, left):
    value = ref[...].T
    turned[...] = value
    left[...] = left_form(value)


def communicate(u_in, l_in, buf, ush, loc, low_t, low_l, up_t, up_l, sems):
    blk = lax.axis_index("blk")
    y = lax.axis_index("col")
    z, x, c = blk // 8, (blk // 2) % 4, blk % 2
    a, b = x + c * (y - x), y + c * (x - y)

    def dev(zz, xx, yy, cc):
        return ((zz * 4 + xx) * 2 + cc, yy)

    def dev_ab(aa, bb):
        return dev(z, aa + c * (bb - aa), bb + c * (aa - bb), c)

    def region(aa, bb, start=0, rows=Q):
        yy, qq = bb + c * (aa - bb), aa + c * (bb - aa)
        return buf.at[c, yy, pl.ds(qq * Q + start, rows), :]

    pending = []

    def send(src, dst, send_sem, recv_sem, device):
        copy = pltpu.make_async_remote_copy(
            src_ref=src, dst_ref=dst, send_sem=send_sem, recv_sem=recv_sem,
            device_id=device, device_id_type=MESH_ID,
        )
        copy.start()
        return copy

    def arrived(dst, recv_sem):
        pltpu.make_async_copy(dst, dst, recv_sem).wait()

    bar = pltpu.get_barrier_semaphore()
    first = jnp.logical_and(blk == 0, y == 0)
    proxy = jnp.logical_and(blk == 1, y == 0)
    column = jnp.logical_and(x == 0, y == 0)
    head = jnp.logical_and(z == 0, jnp.logical_not(first))
    near_row = jnp.logical_and(c == 0, (x == 0) != (y == 0))
    near = jnp.logical_and(z == 0, jnp.logical_or(near_row, jnp.logical_and(c == 1, column)))
    gets_far = jnp.logical_and(c == 0, blk > 0)
    sends_far = jnp.logical_and(c == 1, blk < 127)
    has_next = blk < 127
    up = z <= 8
    sign = 1 - 2 * (z // 9)
    dist = jnp.where(up, z, 16 - z)
    far2 = jnp.logical_or(dist == 4, z == 6)
    far1 = jnp.logical_or(jnp.logical_or(dist == 2, dist == 4), z == 6)
    far3 = z == 12
    step_in = jnp.where(z == 9, 3, jnp.where(dist % 2 == 1, 1, jnp.where(dist == 4, 4, 2)))
    parent = (z - sign * step_in + 16) % 16
    slot = jnp.where(step_in >= 3, 0, jnp.where(step_in == 2, 1, 2)) + 3 * (z // 9)

    def signal(sem, device):
        pl.semaphore_signal(sem, inc=1, device_id=device, device_id_type=MESH_ID)

    def each_peer(act):
        for d in (1, 2, 3):
            act(dev_ab((a + d) % 4, b))
            act(dev_ab(a, (b + d) % 4))
        act(dev(z, x, y, 1 - c))

    @pl.when(jnp.logical_not(first))
    def _():
        each_peer(lambda device: signal(bar, device))

    @pl.when(sends_far)
    def _():
        signal(bar, (blk + 1, y))

    @pl.when(head)
    def _():
        for h in HUBS:
            signal(bar, dev(h, x, y, c))

    @pl.when(proxy)
    def _():
        for h in HUBS:
            signal(bar, dev(h, x, y, 0))

    @pl.when(far3)
    def _():
        signal(bar, dev(9, x, y, c))

    @pl.when(far2)
    def _():
        signal(bar, dev(z + 2 * sign, x, y, c))

    @pl.when(far1)
    def _():
        signal(bar, dev(z + sign, x, y, c))

    local_l = pltpu.make_async_copy(l_in, loc, sems["loc"])
    local_l.start()
    pl.semaphore_wait(
        bar, 7 - near.astype(jnp.int32) + gets_far.astype(jnp.int32) + (z > 0).astype(jnp.int32)
    )

    @pl.when(first)
    def _():
        each_peer(lambda device: signal(sems["late"], device))

    @pl.when(z > 0)
    def _():
        lone = jnp.logical_and(jnp.logical_and(column, c == 0), parent == 0).astype(jnp.int32)
        signal(sems["crd"].at[slot + 6 * lone], dev(parent, x, y, c + lone))

    @pl.when(gets_far)
    def _():
        signal(sems["sh_c"], (blk - 1, y))

    shift = pltpu.make_async_remote_copy(
        src_ref=u_in, dst_ref=ush, send_sem=sems["sh_s"], recv_sem=sems["sh_r"],
        device_id=(jnp.minimum(blk + 1, 127), y), device_id_type=MESH_ID,
    )

    def start_shift():
        @pl.when(sends_far)
        def _():
            pl.semaphore_wait(sems["sh_c"], 1)

        @pl.when(has_next)
        def _():
            shift.start()

    @pl.when(z > 0)
    def _():
        start_shift()

    own = region(a, b)
    root = jnp.logical_and(z == 0, x == 0)

    def scatter_from(src_ref):
        for d in (2, 1, 3):
            rows = pl.ds(d * Q, Q)
            send(src_ref.at[rows, :], buf.at[c, y, rows, :], sems["a_s"].at[d - 1], sems["own_r"],
                 dev(0, d, y, c))
        pltpu.make_async_copy(src_ref.at[pl.ds(0, Q), :], buf.at[c, y, pl.ds(0, Q), :], sems["own_r"]).start()

    @pl.when(jnp.logical_and(root, c == 0))
    def _():
        scatter_from(u_in)

    @pl.when(jnp.logical_and(root, c == 1))
    def _():
        scatter_from(l_in)

    arrived(own, sems["own_r"])

    lone_piece = buf.at[0, 0, pl.ds(0, Q), :]

    def to_child(piece, core, base, i, child):
        pl.semaphore_wait(sems["crd"].at[base + i], 1)
        send(piece, piece, sems["b_s"].at[base + i], sems["own_r"], dev(child, x, y, core))

    def from_root(picks):
        for i in picks:
            to_child(own, c, 0, i, HUBS[i])

    def from_proxy(picks):
        for i in picks:
            to_child(lone_piece, 0, 6, i, HUBS[i])

    @pl.when(head)
    def _():
        from_root((0, 1, 2))

    @pl.when(proxy)
    def _():
        arrived(lone_piece, sems["pt_r"].at[0])
        from_proxy((0, 1, 2))

    side = 3 * (z // 9)

    @pl.when(far3)
    def _():
        to_child(own, c, 0, 3, 9)

    @pl.when(far2)
    def _():
        to_child(own, c, 0, 1 + side, z + 2 * sign)

    @pl.when(far1)
    def _():
        to_child(own, c, 0, 2 + side, z + sign)

    def to_a(d):
        send(own, own, sems["c1_s"].at[d - 1], sems["c1_r"].at[d - 1], dev_ab((a + d) % 4, b))

    def to_b(j):
        piece = region((a + 4 - j) % 4, b)
        send(piece, piece, sems["hp_s"].at[j], sems["hp_r"].at[j], dev_ab(a, (b + 2) % 4))
        send(piece, piece, sems["fp_s"].at[j], sems["fp_r"].at[j], dev_ab(a, (b + 1) % 4))
        send(piece, piece, sems["fm_s"].at[j], sems["fm_r"].at[j], dev_ab(a, (b + 3) % 4))

    def to_partner(aa, bb, index):
        piece = region(aa, bb)
        send(piece, piece, sems["pt_s"].at[index], sems["pt_r"].at[index], dev(z, x, y, 1 - c))

    def took_b(j, d, name):
        aj, bd = (a + 4 - j) % 4, (b + 4 - d) % 4
        arrived(region(aj, bd), sems[name].at[j])
        to_partner(aj, bd, 4 * d + j)

    def took_a(d):
        arrived(region((a + 4 - d) % 4, b), sems["c1_r"].at[d - 1])
        to_b(d)
        to_partner((a + 4 - d) % 4, b, d)

    @pl.when(near)
    def _():
        pl.semaphore_wait(sems["late"], 1)

    to_partner(a, b, 0)
    for d in (2, 1, 3):
        to_a(d)
    to_b(0)

    @pl.when(head)
    def _():
        from_root((3, 4, 5))

    @pl.when(proxy)
    def _():
        from_proxy((3, 4, 5))

    @pl.when(z == 0)
    def _():
        start_shift()

    @pl.when(blk == 0)
    def _():
        ush[...] = jnp.zeros_like(ush)

    local_l.wait()
    prepare(loc, low_t, low_l)
    for d in (3, 1, 2):
        took_a(d)

    @pl.when(blk > 0)
    def _():
        arrived(ush, sems["sh_r"])

    prepare(ush, up_t, up_l)
    for j in (0, 3, 1, 2):
        took_b(j, 1, "fp_r")
        took_b(j, 3, "fm_r")
        took_b(j, 2, "hp_r")

    e = 1 - c
    pa, pb = x + e * (y - x), y + e * (x - y)
    for index in range(16):
        j, d = index % 4, index // 4
        aa, bb = (pa + 4 - j) % 4, (pb + 4 - d) % 4
        yy, qq = bb + e * (aa - bb), aa + e * (bb - aa)
        piece = buf.at[e, yy, pl.ds(qq * Q, Q), :]
        if index == 0:

            @pl.when(jnp.logical_not(proxy))
            def _():
                arrived(piece, sems["pt_r"].at[index])
        else:
            arrived(piece, sems["pt_r"].at[index])

    def finish():
        def sent(ref, sem):
            pltpu.make_async_copy(ref, ref, sem).wait()

        full = region(0, 0)
        for j in range(4):
            sent(full, sems["fp_s"].at[j])
            sent(full, sems["fm_s"].at[j])
            sent(full, sems["hp_s"].at[j])
        for j in range(3):
            sent(full, sems["c1_s"].at[j])
        for j in range(16):
            sent(full, sems["pt_s"].at[j])

        @pl.when(root)
        def _():
            for j in range(3):
                sent(full, sems["a_s"].at[j])

        @pl.when(head)
        def _():
            for j in range(6):
                sent(full, sems["b_s"].at[j])

        @pl.when(proxy)
        def _():
            for j in range(6, 12):
                sent(full, sems["b_s"].at[j])

        @pl.when(far3)
        def _():
            sent(full, sems["b_s"].at[3])

        @pl.when(far2)
        def _():
            sent(full, sems["b_s"].at[1 + side])

        @pl.when(far1)
        def _():
            sent(full, sems["b_s"].at[2 + side])

        @pl.when(has_next)
        def _():
            sent(ush, sems["sh_s"])

    finish()


def compute(buf, low_t, low_l, up_t, up_l, u_out, l_out, n_l, n_r, g_l, h_f, h_l, m_r, k_l, k_n, k_t, d_r):
    rows = lax.broadcasted_iota(jnp.int32, (B, W), 0)
    cols = lax.broadcasted_iota(jnp.int32, (B, W), 1)
    total = jnp.zeros((1, 1), F32)
    for y in range(4):
        f = buf[0, y]
        total = total + jnp.sum(f * f, keepdims=True)
    scale = jnp.sqrt(total / B + 1e-06)
    inv = 1.0 / scale

    def put_left(ref, span, value_hi, value_lo, at):
        ref[span, pl.ds(at, W)] = value_hi
        ref[span, pl.ds(B + at, W)] = value_lo
        ref[span, pl.ds(2 * B + at, W)] = value_hi

    whole = pl.ds(0, B)
    for y in range(4):
        at = y * W
        n = jnp.where(rows == cols + at, 1.0, 0.0) - buf[0, y] * inv
        hi, lo = split(n)
        put_left(n_l, whole, hi, lo, at)
        n_r[pl.ds(0, B), pl.ds(at, W)] = hi
        n_r[pl.ds(B, B), pl.ds(at, W)] = hi
        n_r[pl.ds(2 * B, B), pl.ds(at, W)] = lo
        hi, lo = split(buf[1, y])
        put_left(g_l, whole, hi, lo, at)

    step = 512

    def first(i, carry):
        at = pl.multiple_of(i * step, step)
        span = pl.ds(at, step)
        g = jnp.concatenate([buf[1, y, span, :] for y in range(4)], axis=1)
        h = g + dot_nn(g_l[span, :], n_r[...])
        h_f[span, :] = h
        h_l[span, :] = left_form(h)
        hi, lo = split(dot_nn(n_l[span, :], n_r[...]))
        m_r[span, :] = hi
        m_r[pl.ds(B + at, step), :] = hi
        m_r[pl.ds(2 * B + at, step), :] = lo
        return carry

    lax.fori_loop(0, B // step, first, 0)

    def second(i, carry):
        at = pl.multiple_of(i * step, step)
        span = pl.ds(at, step)
        k = (h_f[span, :] + dot_nn(h_l[span, :], m_r[...])) * inv
        hi, lo = split(k)
        k_n[span, :] = hi
        k_n[pl.ds(B + at, step), :] = hi
        k_n[pl.ds(2 * B + at, step), :] = lo
        k_l[span, :] = jnp.concatenate([hi, lo, hi], axis=1)
        k_t[span, :] = jnp.concatenate([hi, hi, lo], axis=1)
        return carry

    lax.fori_loop(0, B // step, second, 0)

    def third(i, carry):
        at = pl.multiple_of(i * step, step)
        span = pl.ds(at, step)
        hi, lo = split(dot_nt(k_l[span, :], k_t[...]))
        d_r[span, :] = hi
        d_r[pl.ds(B + at, step), :] = hi
        d_r[pl.ds(2 * B + at, step), :] = lo
        return carry

    lax.fori_loop(0, B // step, third, 0)

    mixed = up_t[...] - dot_nn(low_l[...], k_n[...])
    rest = low_t[...] - dot_nt(up_l[...], k_t[...])
    pulled = dot_nt(left_form(mixed), k_t[...])
    both = jnp.concatenate([rest, pulled], axis=0)
    part = 0.3125 * both + 0.0625 * dot_nn(left_form(both), d_r[...])
    part = 0.375 * both + dot_nn(left_form(part), d_r[...])
    part = 0.5 * both + dot_nn(left_form(part), d_r[...])
    u_out[...] = (mixed + dot_nn(left_form(part[W:]), k_n[...])).T
    l_out[...] = (rest + dot_nn(left_form(part[:W]), d_r[...])).T


REG, REG16 = "one", "many"
HUBS = (4, 2, 1, 12, 14, 15)
SEMS = {
    "late": REG, "sh_c": REG, "crd": REG16, "loc": (), "sh_s": (), "sh_r": (), "own_r": (),
    "a_s": (3,), "b_s": (12,), "c1_s": (3,), "c1_r": (3,),
    "fp_s": (4,), "fp_r": (4,), "fm_s": (4,), "fm_r": (4,),
    "hp_s": (4,), "hp_r": (4,),
    "pt_s": (16,), "pt_r": (16,),
}


def kernel(u_in, l_in, u_out, l_out, buf, ush, loc, *rest):
    own, mats, sems = rest[:4], rest[4:14], dict(zip(SEMS, rest[14:]))
    communicate(u_in, l_in, buf, ush, loc, *own, sems)
    compute(buf, *own, u_out, l_out, *mats)


def hold(value):
    return pltpu.with_memory_space_constraint(value.reshape(B, W), pltpu.HBM)


def shards(upper_row, lower_row):
    cat_l, cat_r = pltpu.VMEM((B, 3 * B), BF16), pltpu.VMEM((3 * B, B), BF16)
    kinds = {REG: pltpu.SemaphoreType.REGULAR, REG16: pltpu.SemaphoreType.REGULAR((16,))}
    sems = [kinds[s] if s in kinds else pltpu.SemaphoreType.DMA(s) for s in SEMS.values()]
    new_upper, new_lower = pl.pallas_call(
        kernel,
        out_shape=(pltpu.VMEM((B, W), F32), pltpu.VMEM((B, W), F32)),
        in_specs=[pl.BlockSpec(memory_space=pl.ANY)] * 2,
        out_specs=[pl.BlockSpec(memory_space=pltpu.VMEM)] * 2,
        scratch_shapes=[
            pltpu.VMEM((2, 4, B, W), F32), pltpu.VMEM((B, W), F32), pltpu.VMEM((B, W), F32),
            *[pltpu.VMEM((W, B), F32), pltpu.VMEM((W, 3 * B), BF16)] * 2,
            cat_l, cat_r, cat_l, pltpu.VMEM((B, B), F32), cat_l, cat_r, cat_l, cat_r, cat_l, cat_r,
            *sems,
        ],
        compiler_params=pltpu.CompilerParams(
            collective_id=0, has_side_effects=True, vmem_limit_bytes=56 * 1024 * 1024
        ),
        name="schur",
    )(hold(upper_row), hold(lower_row))
    return new_upper.reshape(B, 1, W), new_lower.reshape(B, 1, W)


def solution(mesh):
    spec = P(None, "blk", "col")
    return jax.shard_map(
        shards, mesh=mesh, in_specs=(spec, spec), out_specs=(spec, spec), check_vma=False
    )
```

```python
import jax
import jax.numpy as jnp
from jax import lax
from jax.experimental import pallas as pl
from jax.experimental.pallas import tpu as pltpu
from jax.sharding import PartitionSpec as P

MESH_ID = pl.DeviceIdType.MESH
F32 = jnp.float32
BF16 = jnp.bfloat16
B = 512
W = 128
Q = 128
NT = (((1,), (1,)), ((), ()))


def split(value):
    hi = value.astype(BF16)
    lo = (value - hi.astype(F32)).astype(BF16)
    return hi, lo


def left_form(value):
    hi, lo = split(value)
    return jnp.concatenate([hi, lo, hi], axis=1)


def dot_nn(left, right):
    return jnp.dot(left, right, preferred_element_type=F32)


def dot_nt(left, right):
    return lax.dot_general(left, right, NT, preferred_element_type=F32)


def prepare(ref, turned, left):
    value = ref[...].T
    turned[...] = value
    left[...] = left_form(value)


def communicate(u_in, l_in, buf, ush, loc, low_t, low_l, up_t, up_l, sems):
    blk = lax.axis_index("blk")
    y = lax.axis_index("col")
    z, x, c = blk // 8, (blk // 2) % 4, blk % 2
    a, b = x + c * (y - x), y + c * (x - y)

    def dev(zz, xx, yy, cc):
        return ((zz * 4 + xx) * 2 + cc, yy)

    def dev_ab(aa, bb):
        return dev(z, aa + c * (bb - aa), bb + c * (aa - bb), c)

    def region(aa, bb, start=0, rows=Q):
        yy, qq = bb + c * (aa - bb), aa + c * (bb - aa)
        return buf.at[c, yy, pl.ds(qq * Q + start, rows), :]

    pending = []

    def send(src, dst, send_sem, recv_sem, device):
        copy = pltpu.make_async_remote_copy(
            src_ref=src, dst_ref=dst, send_sem=send_sem, recv_sem=recv_sem,
            device_id=device, device_id_type=MESH_ID,
        )
        copy.start()
        return copy

    def arrived(dst, recv_sem):
        pltpu.make_async_copy(dst, dst, recv_sem).wait()

    bar = pltpu.get_barrier_semaphore()
    first = jnp.logical_and(blk == 0, y == 0)
    proxy = jnp.logical_and(blk == 1, y == 0)
    column = jnp.logical_and(x == 0, y == 0)
    head = jnp.logical_and(z == 0, jnp.logical_not(first))
    near_row = jnp.logical_and(c == 0, (x == 0) != (y == 0))
    near = jnp.logical_and(z == 0, jnp.logical_or(near_row, jnp.logical_and(c == 1, column)))
    gets_far = jnp.logical_and(c == 0, blk > 0)
    sends_far = jnp.logical_and(c == 1, blk < 127)
    has_next = blk < 127
    up = z <= 8
    sign = 1 - 2 * (z // 9)
    dist = jnp.where(up, z, 16 - z)
    far2 = jnp.logical_or(dist == 4, z == 6)
    far1 = jnp.logical_or(jnp.logical_or(dist == 2, dist == 4), z == 6)
    far3 = z == 12
    step_in = jnp.where(z == 9, 3, jnp.where(dist % 2 == 1, 1, jnp.where(dist == 4, 4, 2)))
    parent = (z - sign * step_in + 16) % 16
    slot = jnp.where(step_in >= 3, 0, jnp.where(step_in == 2, 1, 2)) + 3 * (z // 9)

    def signal(sem, device):
        pl.semaphore_signal(sem, inc=1, device_id=device, device_id_type=MESH_ID)

    def each_peer(act):
        for d in (1, 2, 3):
            act(dev_ab((a + d) % 4, b))
            act(dev_ab(a, (b + d) % 4))
        act(dev(z, x, y, 1 - c))

    @pl.when(jnp.logical_not(first))
    def _():
        each_peer(lambda device: signal(bar, device))

    @pl.when(sends_far)
    def _():
        signal(bar, (blk + 1, y))

    @pl.when(head)
    def _():
        for h in HUBS:
            signal(bar, dev(h, x, y, c))

    @pl.when(proxy)
    def _():
        for h in HUBS:
            signal(bar, dev(h, x, y, 0))

    @pl.when(far3)
    def _():
        signal(bar, dev(9, x, y, c))

    @pl.when(far2)
    def _():
        signal(bar, dev(z + 2 * sign, x, y, c))

    @pl.when(far1)
    def _():
        signal(bar, dev(z + sign, x, y, c))

    local_l = pltpu.make_async_copy(l_in, loc, sems["loc"])
    local_l.start()
    pl.semaphore_wait(
        bar, 7 - near.astype(jnp.int32) + gets_far.astype(jnp.int32) + (z > 0).astype(jnp.int32)
    )

    @pl.when(first)
    def _():
        each_peer(lambda device: signal(sems["late"], device))

    @pl.when(z > 0)
    def _():
        lone = jnp.logical_and(jnp.logical_and(column, c == 0), parent == 0).astype(jnp.int32)
        signal(sems["crd"].at[slot + 6 * lone], dev(parent, x, y, c + lone))

    @pl.when(gets_far)
    def _():
        signal(sems["sh_c"], (blk - 1, y))

    shift = pltpu.make_async_remote_copy(
        src_ref=u_in, dst_ref=ush, send_sem=sems["sh_s"], recv_sem=sems["sh_r"],
        device_id=(jnp.minimum(blk + 1, 127), y), device_id_type=MESH_ID,
    )

    def start_shift():
        @pl.when(sends_far)
        def _():
            pl.semaphore_wait(sems["sh_c"], 1)

        @pl.when(has_next)
        def _():
            shift.start()

    @pl.when(z > 0)
    def _():
        start_shift()

    own = region(a, b)
    root = jnp.logical_and(z == 0, x == 0)

    def scatter_from(src_ref):
        for d in (2, 1, 3):
            rows = pl.ds(d * Q, Q)
            send(src_ref.at[rows, :], buf.at[c, y, rows, :], sems["a_s"].at[d - 1], sems["own_r"],
                 dev(0, d, y, c))
        pltpu.make_async_copy(src_ref.at[pl.ds(0, Q), :], buf.at[c, y, pl.ds(0, Q), :], sems["own_r"]).start()

    @pl.when(jnp.logical_and(root, c == 0))
    def _():
        scatter_from(u_in)

    @pl.when(jnp.logical_and(root, c == 1))
    def _():
        scatter_from(l_in)

    arrived(own, sems["own_r"])

    lone_piece = buf.at[0, 0, pl.ds(0, Q), :]

    def to_child(piece, core, base, i, child):
        pl.semaphore_wait(sems["crd"].at[base + i], 1)
        send(piece, piece, sems["b_s"].at[base + i], sems["own_r"], dev(child, x, y, core))

    def from_root(picks):
        for i in picks:
            to_child(own, c, 0, i, HUBS[i])

    def from_proxy(picks):
        for i in picks:
            to_child(lone_piece, 0, 6, i, HUBS[i])

    @pl.when(head)
    def _():
        from_root((0, 1, 2))

    @pl.when(proxy)
    def _():
        arrived(lone_piece, sems["pt_r"].at[0])
        from_proxy((0, 1, 2))

    side = 3 * (z // 9)

    @pl.when(far3)
    def _():
        to_child(own, c, 0, 3, 9)

    @pl.when(far2)
    def _():
        to_child(own, c, 0, 1 + side, z + 2 * sign)

    @pl.when(far1)
    def _():
        to_child(own, c, 0, 2 + side, z + sign)

    def to_a(d):
        send(own, own, sems["c1_s"].at[d - 1], sems["c1_r"].at[d - 1], dev_ab((a + d) % 4, b))

    def to_b(j):
        piece = region((a + 4 - j) % 4, b)
        send(piece, piece, sems["hp_s"].at[j], sems["hp_r"].at[j], dev_ab(a, (b + 2) % 4))
        send(piece, piece, sems["fp_s"].at[j], sems["fp_r"].at[j], dev_ab(a, (b + 1) % 4))
        send(piece, piece, sems["fm_s"].at[j], sems["fm_r"].at[j], dev_ab(a, (b + 3) % 4))

    def to_partner(aa, bb, index):
        piece = region(aa, bb)
        send(piece, piece, sems["pt_s"].at[index], sems["pt_r"].at[index], dev(z, x, y, 1 - c))

    def took_b(j, d, name):
        aj, bd = (a + 4 - j) % 4, (b + 4 - d) % 4
        arrived(region(aj, bd), sems[name].at[j])
        to_partner(aj, bd, 4 * d + j)

    def took_a(d):
        arrived(region((a + 4 - d) % 4, b), sems["c1_r"].at[d - 1])
        to_b(d)
        to_partner((a + 4 - d) % 4, b, d)

    @pl.when(near)
    def _():
        pl.semaphore_wait(sems["late"], 1)

    to_partner(a, b, 0)
    for d in (2, 1, 3):
        to_a(d)
    to_b(0)

    @pl.when(head)
    def _():
        from_root((3, 4, 5))

    @pl.when(proxy)
    def _():
        from_proxy((3, 4, 5))

    @pl.when(z == 0)
    def _():
        start_shift()

    @pl.when(blk == 0)
    def _():
        ush[...] = jnp.zeros_like(ush)

    local_l.wait()
    prepare(loc, low_t, low_l)
    for d in (3, 1, 2):
        took_a(d)

    @pl.when(blk > 0)
    def _():
        arrived(ush, sems["sh_r"])

    prepare(ush, up_t, up_l)
    for j in (0, 3, 1, 2):
        took_b(j, 1, "fp_r")
        took_b(j, 3, "fm_r")
        took_b(j, 2, "hp_r")

    e = 1 - c
    pa, pb = x + e * (y - x), y + e * (x - y)
    for index in range(16):
        j, d = index % 4, index // 4
        aa, bb = (pa + 4 - j) % 4, (pb + 4 - d) % 4
        yy, qq = bb + e * (aa - bb), aa + e * (bb - aa)
        piece = buf.at[e, yy, pl.ds(qq * Q, Q), :]
        if index == 0:

            @pl.when(jnp.logical_not(proxy))
            def _():
                arrived(piece, sems["pt_r"].at[index])
        else:
            arrived(piece, sems["pt_r"].at[index])

    def finish():
        def sent(ref, sem):
            pltpu.make_async_copy(ref, ref, sem).wait()

        full = region(0, 0)
        for j in range(4):
            sent(full, sems["fp_s"].at[j])
            sent(full, sems["fm_s"].at[j])
            sent(full, sems["hp_s"].at[j])
        for j in range(3):
            sent(full, sems["c1_s"].at[j])
        for j in range(16):
            sent(full, sems["pt_s"].at[j])

        @pl.when(root)
        def _():
            for j in range(3):
                sent(full, sems["a_s"].at[j])

        @pl.when(head)
        def _():
            for j in range(6):
                sent(full, sems["b_s"].at[j])

        @pl.when(proxy)
        def _():
            for j in range(6, 12):
                sent(full, sems["b_s"].at[j])

        @pl.when(far3)
        def _():
            sent(full, sems["b_s"].at[3])

        @pl.when(far2)
        def _():
            sent(full, sems["b_s"].at[1 + side])

        @pl.when(far1)
        def _():
            sent(full, sems["b_s"].at[2 + side])

        @pl.when(has_next)
        def _():
            sent(ush, sems["sh_s"])

    finish()


def compute(buf, low_t, low_l, up_t, up_l, u_out, l_out, n_l, n_r, g_l, h_f, h_l, m_r, k_l, k_n, k_t, d_r):
    rows = lax.broadcasted_iota(jnp.int32, (B, W), 0)
    cols = lax.broadcasted_iota(jnp.int32, (B, W), 1)
    total = jnp.zeros((1, 1), F32)
    for y in range(4):
        f = buf[0, y]
        total = total + jnp.sum(f * f, keepdims=True)
    scale = jnp.sqrt(total / B + 1e-06)
    inv = 1.0 / scale

    def put_left(ref, span, value_hi, value_lo, at):
        ref[span, pl.ds(at, W)] = value_hi
        ref[span, pl.ds(B + at, W)] = value_lo
        ref[span, pl.ds(2 * B + at, W)] = value_hi

    whole = pl.ds(0, B)
    for y in range(4):
        at = y * W
        n = jnp.where(rows == cols + at, 1.0, 0.0) - buf[0, y] * inv
        hi, lo = split(n)
        put_left(n_l, whole, hi, lo, at)
        n_r[pl.ds(0, B), pl.ds(at, W)] = hi
        n_r[pl.ds(B, B), pl.ds(at, W)] = hi
        n_r[pl.ds(2 * B, B), pl.ds(at, W)] = lo
        hi, lo = split(buf[1, y])
        put_left(g_l, whole, hi, lo, at)

    step = 512

    def first(i, carry):
        at = pl.multiple_of(i * step, step)
        span = pl.ds(at, step)
        g = jnp.concatenate([buf[1, y, span, :] for y in range(4)], axis=1)
        h = g + dot_nn(g_l[span, :], n_r[...])
        h_f[span, :] = h
        h_l[span, :] = left_form(h)
        hi, lo = split(dot_nn(n_l[span, :], n_r[...]))
        m_r[span, :] = hi
        m_r[pl.ds(B + at, step), :] = hi
        m_r[pl.ds(2 * B + at, step), :] = lo
        return carry

    lax.fori_loop(0, B // step, first, 0)

    def second(i, carry):
        at = pl.multiple_of(i * step, step)
        span = pl.ds(at, step)
        k = (h_f[span, :] + dot_nn(h_l[span, :], m_r[...])) * inv
        hi, lo = split(k)
        k_n[span, :] = hi
        k_n[pl.ds(B + at, step), :] = hi
        k_n[pl.ds(2 * B + at, step), :] = lo
        k_l[span, :] = jnp.concatenate([hi, lo, hi], axis=1)
        k_t[span, :] = jnp.concatenate([hi, hi, lo], axis=1)
        return carry

    lax.fori_loop(0, B // step, second, 0)

    def third(i, carry):
        at = pl.multiple_of(i * step, step)
        span = pl.ds(at, step)
        hi, lo = split(dot_nt(k_l[span, :], k_t[...]))
        d_r[span, :] = hi
        d_r[pl.ds(B + at, step), :] = hi
        d_r[pl.ds(2 * B + at, step), :] = lo
        return carry

    lax.fori_loop(0, B // step, third, 0)

    mixed = up_t[...] - dot_nn(low_l[...], k_n[...])
    pair = dot_nt(jnp.concatenate([up_l[...], left_form(mixed)], axis=0), k_t[...])
    rest, pulled = low_t[...] - pair[:W], pair[W:]
    both = jnp.concatenate([rest, pulled], axis=0)
    part = 0.3125 * both + 0.0625 * dot_nn(left_form(both), d_r[...])
    part = 0.375 * both + dot_nn(left_form(part), d_r[...])
    part = 0.5 * both + dot_nn(left_form(part), d_r[...])
    u_out[...] = (mixed + dot_nn(left_form(part[W:]), k_n[...])).T
    l_out[...] = (rest + dot_nn(left_form(part[:W]), d_r[...])).T


REG, REG16 = "one", "many"
HUBS = (4, 2, 1, 12, 14, 15)
SEMS = {
    "late": REG, "sh_c": REG, "crd": REG16, "loc": (), "sh_s": (), "sh_r": (), "own_r": (),
    "a_s": (3,), "b_s": (12,), "c1_s": (3,), "c1_r": (3,),
    "fp_s": (4,), "fp_r": (4,), "fm_s": (4,), "fm_r": (4,),
    "hp_s": (4,), "hp_r": (4,),
    "pt_s": (16,), "pt_r": (16,),
}


def kernel(u_in, l_in, u_out, l_out, buf, ush, loc, *rest):
    own, mats, sems = rest[:4], rest[4:14], dict(zip(SEMS, rest[14:]))
    communicate(u_in, l_in, buf, ush, loc, *own, sems)
    compute(buf, *own, u_out, l_out, *mats)


def hold(value):
    return pltpu.with_memory_space_constraint(value.reshape(B, W), pltpu.HBM)


def shards(upper_row, lower_row):
    cat_l, cat_r = pltpu.VMEM((B, 3 * B), BF16), pltpu.VMEM((3 * B, B), BF16)
    kinds = {REG: pltpu.SemaphoreType.REGULAR, REG16: pltpu.SemaphoreType.REGULAR((16,))}
    sems = [kinds[s] if s in kinds else pltpu.SemaphoreType.DMA(s) for s in SEMS.values()]
    new_upper, new_lower = pl.pallas_call(
        kernel,
        out_shape=(pltpu.VMEM((B, W), F32), pltpu.VMEM((B, W), F32)),
        in_specs=[pl.BlockSpec(memory_space=pl.ANY)] * 2,
        out_specs=[pl.BlockSpec(memory_space=pltpu.VMEM)] * 2,
        scratch_shapes=[
            pltpu.VMEM((2, 4, B, W), F32), pltpu.VMEM((B, W), F32), pltpu.VMEM((B, W), F32),
            *[pltpu.VMEM((W, B), F32), pltpu.VMEM((W, 3 * B), BF16)] * 2,
            cat_l, cat_r, cat_l, pltpu.VMEM((B, B), F32), cat_l, cat_r, cat_l, cat_r, cat_l, cat_r,
            *sems,
        ],
        compiler_params=pltpu.CompilerParams(
            collective_id=0, has_side_effects=True, vmem_limit_bytes=56 * 1024 * 1024
        ),
        name="schur",
    )(hold(upper_row), hold(lower_row))
    return new_upper.reshape(B, 1, W), new_lower.reshape(B, 1, W)


def solution(mesh):
    spec = P(None, "blk", "col")
    return jax.shard_map(
        shards, mesh=mesh, in_specs=(spec, spec), out_specs=(spec, spec), check_vma=False
    )
```

```python
import jax
import jax.numpy as jnp
from jax import lax
from jax.experimental import pallas as pl
from jax.experimental.pallas import tpu as pltpu
from jax.sharding import PartitionSpec as P

MESH_ID = pl.DeviceIdType.MESH
F32 = jnp.float32
BF16 = jnp.bfloat16
B = 512
W = 128
Q = 128
NT = (((1,), (1,)), ((), ()))


def split(value):
    hi = value.astype(BF16)
    lo = (value - hi.astype(F32)).astype(BF16)
    return hi, lo


def left_form(value):
    hi, lo = split(value)
    return jnp.concatenate([hi, lo, hi], axis=1)


def dot_nn(left, right):
    return jnp.dot(left, right, preferred_element_type=F32)


def dot_nt(left, right):
    return lax.dot_general(left, right, NT, preferred_element_type=F32)


def prepare(ref, turned, left):
    value = ref[...].T
    turned[...] = value
    left[...] = left_form(value)


def communicate(u_in, l_in, buf, ush, loc, low_t, low_l, up_t, up_l, sems):
    blk = lax.axis_index("blk")
    y = lax.axis_index("col")
    z, x, c = blk // 8, (blk // 2) % 4, blk % 2
    a, b = x + c * (y - x), y + c * (x - y)

    def dev(zz, xx, yy, cc):
        return ((zz * 4 + xx) * 2 + cc, yy)

    def dev_ab(aa, bb):
        return dev(z, aa + c * (bb - aa), bb + c * (aa - bb), c)

    def region(aa, bb, start=0, rows=Q):
        yy, qq = bb + c * (aa - bb), aa + c * (bb - aa)
        return buf.at[c, yy, pl.ds(qq * Q + start, rows), :]

    pending = []

    def send(src, dst, send_sem, recv_sem, device):
        copy = pltpu.make_async_remote_copy(
            src_ref=src, dst_ref=dst, send_sem=send_sem, recv_sem=recv_sem,
            device_id=device, device_id_type=MESH_ID,
        )
        copy.start()
        return copy

    def arrived(dst, recv_sem):
        pltpu.make_async_copy(dst, dst, recv_sem).wait()

    bar = pltpu.get_barrier_semaphore()
    first = jnp.logical_and(blk == 0, y == 0)
    proxy = jnp.logical_and(blk == 1, y == 0)
    column = jnp.logical_and(x == 0, y == 0)
    head = jnp.logical_and(z == 0, jnp.logical_not(first))
    near_row = jnp.logical_and(c == 0, (x == 0) != (y == 0))
    near = jnp.logical_and(z == 0, jnp.logical_or(near_row, jnp.logical_and(c == 1, column)))
    gets_far = jnp.logical_and(c == 0, blk > 0)
    sends_far = jnp.logical_and(c == 1, blk < 127)
    has_next = blk < 127
    up = z <= 8
    sign = 1 - 2 * (z // 9)
    dist = jnp.where(up, z, 16 - z)
    far2 = jnp.logical_or(dist == 4, z == 6)
    far1 = jnp.logical_or(jnp.logical_or(dist == 2, dist == 4), z == 6)
    far3 = z == 12
    step_in = jnp.where(z == 9, 3, jnp.where(dist % 2 == 1, 1, jnp.where(dist == 4, 4, 2)))
    parent = (z - sign * step_in + 16) % 16
    slot = jnp.where(step_in >= 3, 0, jnp.where(step_in == 2, 1, 2)) + 3 * (z // 9)

    def signal(sem, device):
        pl.semaphore_signal(sem, inc=1, device_id=device, device_id_type=MESH_ID)

    def each_peer(act):
        for d in (1, 2, 3):
            act(dev_ab((a + d) % 4, b))
            act(dev_ab(a, (b + d) % 4))
        act(dev(z, x, y, 1 - c))

    @pl.when(jnp.logical_not(first))
    def _():
        each_peer(lambda device: signal(bar, device))

    @pl.when(sends_far)
    def _():
        signal(bar, (blk + 1, y))

    @pl.when(head)
    def _():
        for h in HUBS:
            signal(bar, dev(h, x, y, c))

    @pl.when(proxy)
    def _():
        for h in HUBS:
            signal(bar, dev(h, x, y, 0))

    @pl.when(far3)
    def _():
        signal(bar, dev(9, x, y, c))

    @pl.when(far2)
    def _():
        signal(bar, dev(z + 2 * sign, x, y, c))

    @pl.when(far1)
    def _():
        signal(bar, dev(z + sign, x, y, c))

    local_l = pltpu.make_async_copy(l_in, loc, sems["loc"])
    local_l.start()
    pl.semaphore_wait(
        bar, 7 - near.astype(jnp.int32) + gets_far.astype(jnp.int32) + (z > 0).astype(jnp.int32)
    )

    @pl.when(first)
    def _():
        each_peer(lambda device: signal(sems["late"], device))

    @pl.when(z > 0)
    def _():
        lone = jnp.logical_and(jnp.logical_and(column, c == 0), parent == 0).astype(jnp.int32)
        signal(sems["crd"].at[slot + 6 * lone], dev(parent, x, y, c + lone))

    @pl.when(gets_far)
    def _():
        signal(sems["sh_c"], (blk - 1, y))

    shift = pltpu.make_async_remote_copy(
        src_ref=u_in, dst_ref=ush, send_sem=sems["sh_s"], recv_sem=sems["sh_r"],
        device_id=(jnp.minimum(blk + 1, 127), y), device_id_type=MESH_ID,
    )

    def start_shift():
        @pl.when(sends_far)
        def _():
            pl.semaphore_wait(sems["sh_c"], 1)

        @pl.when(has_next)
        def _():
            shift.start()

    @pl.when(z > 0)
    def _():
        start_shift()

    own = region(a, b)
    root = jnp.logical_and(z == 0, x == 0)

    def scatter_from(src_ref):
        for d in (2, 1, 3):
            rows = pl.ds(d * Q, Q)
            send(src_ref.at[rows, :], buf.at[c, y, rows, :], sems["a_s"].at[d - 1], sems["own_r"],
                 dev(0, d, y, c))
        pltpu.make_async_copy(src_ref.at[pl.ds(0, Q), :], buf.at[c, y, pl.ds(0, Q), :], sems["own_r"]).start()

    @pl.when(jnp.logical_and(root, c == 0))
    def _():
        scatter_from(u_in)

    @pl.when(jnp.logical_and(root, c == 1))
    def _():
        scatter_from(l_in)

    arrived(own, sems["own_r"])

    lone_piece = buf.at[0, 0, pl.ds(0, Q), :]

    def to_child(piece, core, base, i, child):
        pl.semaphore_wait(sems["crd"].at[base + i], 1)
        send(piece, piece, sems["b_s"].at[base + i], sems["own_r"], dev(child, x, y, core))

    def from_root(picks):
        for i in picks:
            to_child(own, c, 0, i, HUBS[i])

    def from_proxy(picks):
        for i in picks:
            to_child(lone_piece, 0, 6, i, HUBS[i])

    @pl.when(head)
    def _():
        from_root((0, 1, 2))

    @pl.when(proxy)
    def _():
        arrived(lone_piece, sems["pt_r"].at[0])
        from_proxy((0, 1, 2))

    side = 3 * (z // 9)

    @pl.when(far3)
    def _():
        to_child(own, c, 0, 3, 9)

    @pl.when(far2)
    def _():
        to_child(own, c, 0, 1 + side, z + 2 * sign)

    @pl.when(far1)
    def _():
        to_child(own, c, 0, 2 + side, z + sign)

    def to_a(d):
        send(own, own, sems["c1_s"].at[d - 1], sems["c1_r"].at[d - 1], dev_ab((a + d) % 4, b))

    def to_b(j):
        piece = region((a + 4 - j) % 4, b)
        send(piece, piece, sems["hp_s"].at[j], sems["hp_r"].at[j], dev_ab(a, (b + 2) % 4))
        send(piece, piece, sems["fp_s"].at[j], sems["fp_r"].at[j], dev_ab(a, (b + 1) % 4))
        send(piece, piece, sems["fm_s"].at[j], sems["fm_r"].at[j], dev_ab(a, (b + 3) % 4))

    def to_partner(aa, bb, index):
        piece = region(aa, bb)
        send(piece, piece, sems["pt_s"].at[index], sems["pt_r"].at[index], dev(z, x, y, 1 - c))

    def took_b(j, d, name):
        aj, bd = (a + 4 - j) % 4, (b + 4 - d) % 4
        arrived(region(aj, bd), sems[name].at[j])
        to_partner(aj, bd, 4 * d + j)

    def took_a(d):
        arrived(region((a + 4 - d) % 4, b), sems["c1_r"].at[d - 1])
        to_b(d)
        to_partner((a + 4 - d) % 4, b, d)

    @pl.when(near)
    def _():
        pl.semaphore_wait(sems["late"], 1)

    to_partner(a, b, 0)
    for d in (2, 1, 3):
        to_a(d)
    to_b(0)

    @pl.when(head)
    def _():
        from_root((3, 4, 5))

    @pl.when(proxy)
    def _():
        from_proxy((3, 4, 5))

    @pl.when(z == 0)
    def _():
        start_shift()

    @pl.when(blk == 0)
    def _():
        ush[...] = jnp.zeros_like(ush)

    local_l.wait()
    prepare(loc, low_t, low_l)
    for d in (3, 1, 2):
        took_a(d)

    @pl.when(blk > 0)
    def _():
        arrived(ush, sems["sh_r"])

    prepare(ush, up_t, up_l)
    for j in (0, 3, 1, 2):
        took_b(j, 1, "fp_r")
        took_b(j, 3, "fm_r")
        took_b(j, 2, "hp_r")

    e = 1 - c
    pa, pb = x + e * (y - x), y + e * (x - y)
    for index in range(16):
        j, d = index % 4, index // 4
        aa, bb = (pa + 4 - j) % 4, (pb + 4 - d) % 4
        yy, qq = bb + e * (aa - bb), aa + e * (bb - aa)
        piece = buf.at[e, yy, pl.ds(qq * Q, Q), :]
        if index == 0:

            @pl.when(jnp.logical_not(proxy))
            def _():
                arrived(piece, sems["pt_r"].at[index])
        else:
            arrived(piece, sems["pt_r"].at[index])

    def finish():
        def sent(ref, sem):
            pltpu.make_async_copy(ref, ref, sem).wait()

        full = region(0, 0)
        for j in range(4):
            sent(full, sems["fp_s"].at[j])
            sent(full, sems["fm_s"].at[j])
            sent(full, sems["hp_s"].at[j])
        for j in range(3):
            sent(full, sems["c1_s"].at[j])
        for j in range(16):
            sent(full, sems["pt_s"].at[j])

        @pl.when(root)
        def _():
            for j in range(3):
                sent(full, sems["a_s"].at[j])

        @pl.when(head)
        def _():
            for j in range(6):
                sent(full, sems["b_s"].at[j])

        @pl.when(proxy)
        def _():
            for j in range(6, 12):
                sent(full, sems["b_s"].at[j])

        @pl.when(far3)
        def _():
            sent(full, sems["b_s"].at[3])

        @pl.when(far2)
        def _():
            sent(full, sems["b_s"].at[1 + side])

        @pl.when(far1)
        def _():
            sent(full, sems["b_s"].at[2 + side])

        @pl.when(has_next)
        def _():
            sent(ush, sems["sh_s"])

    finish()


def compute(buf, low_t, low_l, up_t, up_l, u_out, l_out, n_l, n_r, g_l, h_f, h_l, m_r, k_l, k_n, k_t, d_r):
    rows = lax.broadcasted_iota(jnp.int32, (B, W), 0)
    cols = lax.broadcasted_iota(jnp.int32, (B, W), 1)
    total = jnp.zeros((1, 1), F32)
    for y in range(4):
        f = buf[0, y]
        total = total + jnp.sum(f * f, keepdims=True)
    scale = jnp.sqrt(total / B + 1e-06)
    inv = 1.0 / scale

    def put_left(ref, span, value_hi, value_lo, at):
        ref[span, pl.ds(at, W)] = value_hi
        ref[span, pl.ds(B + at, W)] = value_lo
        ref[span, pl.ds(2 * B + at, W)] = value_hi

    whole = pl.ds(0, B)
    for y in range(4):
        at = y * W
        n = jnp.where(rows == cols + at, 1.0, 0.0) - buf[0, y] * inv
        hi, lo = split(n)
        put_left(n_l, whole, hi, lo, at)
        n_r[pl.ds(0, B), pl.ds(at, W)] = hi
        n_r[pl.ds(B, B), pl.ds(at, W)] = hi
        n_r[pl.ds(2 * B, B), pl.ds(at, W)] = lo
        hi, lo = split(buf[1, y])
        put_left(g_l, whole, hi, lo, at)

    step = 512

    def first(i, carry):
        at = pl.multiple_of(i * step, step)
        span = pl.ds(at, step)
        g = jnp.concatenate([buf[1, y, span, :] for y in range(4)], axis=1)
        pair = dot_nn(jnp.concatenate([g_l[span, :], n_l[span, :]], axis=0), n_r[...])
        h = g + pair[:step]
        h_f[span, :] = h
        h_l[span, :] = left_form(h)
        hi, lo = split(pair[step:])
        m_r[span, :] = hi
        m_r[pl.ds(B + at, step), :] = hi
        m_r[pl.ds(2 * B + at, step), :] = lo
        return carry

    lax.fori_loop(0, B // step, first, 0)

    def second(i, carry):
        at = pl.multiple_of(i * step, step)
        span = pl.ds(at, step)
        k = (h_f[span, :] + dot_nn(h_l[span, :], m_r[...])) * inv
        hi, lo = split(k)
        k_n[span, :] = hi
        k_n[pl.ds(B + at, step), :] = hi
        k_n[pl.ds(2 * B + at, step), :] = lo
        k_l[span, :] = jnp.concatenate([hi, lo, hi], axis=1)
        k_t[span, :] = jnp.concatenate([hi, hi, lo], axis=1)
        return carry

    lax.fori_loop(0, B // step, second, 0)

    def third(i, carry):
        at = pl.multiple_of(i * step, step)
        span = pl.ds(at, step)
        hi, lo = split(dot_nt(k_l[span, :], k_t[...]))
        d_r[span, :] = hi
        d_r[pl.ds(B + at, step), :] = hi
        d_r[pl.ds(2 * B + at, step), :] = lo
        return carry

    lax.fori_loop(0, B // step, third, 0)

    mixed = up_t[...] - dot_nn(low_l[...], k_n[...])
    pair = dot_nt(jnp.concatenate([up_l[...], left_form(mixed)], axis=0), k_t[...])
    rest, pulled = low_t[...] - pair[:W], pair[W:]
    both = jnp.concatenate([rest, pulled], axis=0)
    part = 0.3125 * both + 0.0625 * dot_nn(left_form(both), d_r[...])
    part = 0.375 * both + dot_nn(left_form(part), d_r[...])
    part = 0.5 * both + dot_nn(left_form(part), d_r[...])
    u_out[...] = (mixed + dot_nn(left_form(part[W:]), k_n[...])).T
    l_out[...] = (rest + dot_nn(left_form(part[:W]), d_r[...])).T


REG, REG16 = "one", "many"
HUBS = (4, 2, 1, 12, 14, 15)
SEMS = {
    "late": REG, "sh_c": REG, "crd": REG16, "loc": (), "sh_s": (), "sh_r": (), "own_r": (),
    "a_s": (3,), "b_s": (12,), "c1_s": (3,), "c1_r": (3,),
    "fp_s": (4,), "fp_r": (4,), "fm_s": (4,), "fm_r": (4,),
    "hp_s": (4,), "hp_r": (4,),
    "pt_s": (16,), "pt_r": (16,),
}


def kernel(u_in, l_in, u_out, l_out, buf, ush, loc, *rest):
    own, mats, sems = rest[:4], rest[4:14], dict(zip(SEMS, rest[14:]))
    communicate(u_in, l_in, buf, ush, loc, *own, sems)
    compute(buf, *own, u_out, l_out, *mats)


def hold(value):
    return pltpu.with_memory_space_constraint(value.reshape(B, W), pltpu.HBM)


def shards(upper_row, lower_row):
    cat_l, cat_r = pltpu.VMEM((B, 3 * B), BF16), pltpu.VMEM((3 * B, B), BF16)
    kinds = {REG: pltpu.SemaphoreType.REGULAR, REG16: pltpu.SemaphoreType.REGULAR((16,))}
    sems = [kinds[s] if s in kinds else pltpu.SemaphoreType.DMA(s) for s in SEMS.values()]
    new_upper, new_lower = pl.pallas_call(
        kernel,
        out_shape=(pltpu.VMEM((B, W), F32), pltpu.VMEM((B, W), F32)),
        in_specs=[pl.BlockSpec(memory_space=pl.ANY)] * 2,
        out_specs=[pl.BlockSpec(memory_space=pltpu.VMEM)] * 2,
        scratch_shapes=[
            pltpu.VMEM((2, 4, B, W), F32), pltpu.VMEM((B, W), F32), pltpu.VMEM((B, W), F32),
            *[pltpu.VMEM((W, B), F32), pltpu.VMEM((W, 3 * B), BF16)] * 2,
            cat_l, cat_r, cat_l, pltpu.VMEM((B, B), F32), cat_l, cat_r, cat_l, cat_r, cat_l, cat_r,
            *sems,
        ],
        compiler_params=pltpu.CompilerParams(
            collective_id=0, has_side_effects=True, vmem_limit_bytes=56 * 1024 * 1024
        ),
        name="schur",
    )(hold(upper_row), hold(lower_row))
    return new_upper.reshape(B, 1, W), new_lower.reshape(B, 1, W)


def solution(mesh):
    spec = P(None, "blk", "col")
    return jax.shard_map(
        shards, mesh=mesh, in_specs=(spec, spec), out_specs=(spec, spec), check_vma=False
    )
```
